512 devices in a mesh: rows: 32 (over z, x), piv: 16 (over y, core).
Axes of the slice: x: 4, y: 8, z: 8, core: 2. Of those that a mesh axis runs over, the one named last changes fastest.
Arguments:
- ancestor_sol: float32 [1024, 32768], P('piv', 'rows'), may hold values from -6 to 6
- front_map: int32 [256], P('rows'), may hold values from 0 to 255, each once
- lower_panel: float32 [32768, 12288], P('rows', 'piv'), may hold values from -0.03125 to 0.03125
- inverse_factor: float32 [12288, 12288], P('piv', 'rows'), as said below
- right_side: float32 [1024, 12288], P(None, ('piv', 'rows')), may hold values from -6 to 6
- child_start: int32 [128], P('rows'), may hold values from 0 to 12287, as said below
- child_len: int32 [128], P('rows'), may hold values from 1 to 128, as said below
Outputs:
- child_blocks: float32 [1024, 16384], P('piv', 'rows')
The draws below stay inside these ranges and needn't reach their ends.
Inputs may be any that keep to these rules, and one draw needn't show every extreme that they name: Child block c lies within pivots k * 384 to (k + 1) * 384 - 1, with k = c // 4; child_start[c] + child_len[c] <= (k + 1) * 384. `child_len`: child block 0 is full. inverse_factor is lower triangular with a diagonal in [0.5, 2].
All inputs are finite; a program needn't handle non-finite values.
Results may differ from the reference program's by a relative error of at most 0.000088.
Values sent between devices are 32-bit elements; how exact they have to be, the bound alone decides.
No kernel may reach another device: no remote copies, remote signals or barrier semaphores. Data moves between devices by JAX's collectives and lax.ppermute only.
A program may use at most 64 MiB of HBM per device.

```python
import jax
import jax.numpy as jnp
from jax import lax

PIVOTS = 12288
SOURCES = 1024
ROW_BLK = 128
CHILD_BLK = 128
CB_DEV = 4
NFB = 256
BOUNDARY = 32768
NCB = 128
PIV_ROWS = 384


def child_pair(key):
    base = jax.random.fold_in(key, 4242)
    first, second = jax.random.split(base)
    lowest = CHILD_BLK // 4 + 1
    lengths = jax.random.randint(first, (NCB,), lowest, CHILD_BLK + 1).astype(jnp.int32)
    lengths = lengths.at[0].set(CHILD_BLK)
    owner = jnp.arange(NCB, dtype=jnp.int32) // CB_DEV
    room = PIV_ROWS - lengths + 1
    offset = jax.random.randint(second, (NCB,), 0, 1 << 20).astype(jnp.int32) % room
    return (owner * PIV_ROWS + offset, lengths)


def draw_child_start(key, part):
    return child_pair(key)[0]


def draw_child_len(key, part):
    return child_pair(key)[1]


def draw_inverse_factor(key, part):
    first, second = jax.random.split(jax.random.fold_in(key, 77))
    rowpos = jnp.arange(PIVOTS)[:, None]
    colpos = jnp.arange(PIVOTS)[None, :]
    values = jax.random.normal(first, (PIVOTS, PIVOTS), jnp.float32) * PIVOTS ** (-0.5)
    diagonal = jax.random.uniform(second, (PIVOTS,), jnp.float32, 0.5, 2.0)
    lower = jnp.where(rowpos > colpos, values, jnp.zeros_like(values))
    return lower + jnp.diag(diagonal)


def steps_of(own_key, extent, cuts, least, top_value):
    factor_of = 1.0
    for dim, shards_of in cuts:
        heights = jax.random.uniform(jax.random.fold_in(jax.random.fold_in(own_key, 6), dim), (shards_of,), jnp.float32, least / len(cuts), top_value / len(cuts))
        factor_of = factor_of * jnp.repeat(jnp.exp(heights), extent[dim] // shards_of).reshape((-1,) + (1,) * (len(extent) - 1 - dim))
    return factor_of


def bell_draw(stream_key, extent, deviation, reach, cuts=(), kind=jnp.bfloat16):
    entries = deviation * jax.random.normal(stream_key, extent, jnp.float32)
    if cuts:
        entries = entries * steps_of(stream_key, extent, cuts, -0.22, 0.18)
    return jnp.clip(entries, -reach, reach).astype(kind)


def setup_inputs(seed: int = 0) -> dict:
    key_list = jax.random.split(jax.random.key(seed), 8)
    return {
        "ancestor_sol": bell_draw(key_list[0], (SOURCES, BOUNDARY), 1.0, 6.0, ((0, 16), (1, 32)), jnp.float32),
        "front_map": jax.random.permutation(key_list[1], NFB).astype(jnp.int32),
        "lower_panel": bell_draw(key_list[2], (BOUNDARY, PIVOTS), BOUNDARY ** -0.5, 0.03125, ((0, 32), (1, 16)), jnp.float32),
        "inverse_factor": draw_inverse_factor(jax.random.fold_in(key_list[7], 71), 0),
        "right_side": bell_draw(key_list[4], (SOURCES, PIVOTS), 1.0, 6.0, ((1, 512),), jnp.float32),
        "child_start": draw_child_start(jax.random.fold_in(key_list[7], 71), 0),
        "child_len": draw_child_len(jax.random.fold_in(key_list[7], 71), 0),
    }


def reference(ancestor_sol, front_map, lower_panel, inverse_factor, right_side, child_start, child_len):
    blocks = ancestor_sol.reshape(SOURCES, NFB, ROW_BLK)
    boundary = jnp.take(blocks, front_map.astype(jnp.int32), axis=1).reshape(SOURCES, NFB * ROW_BLK)
    coupled = jnp.dot(boundary, lower_panel, precision=lax.Precision.HIGHEST, preferred_element_type=jnp.float32)
    reduced = right_side - coupled
    solution = jnp.dot(reduced, inverse_factor, precision=lax.Precision.HIGHEST, preferred_element_type=jnp.float32)
    slots = jnp.arange(CHILD_BLK, dtype=jnp.int32)
    index = child_start.astype(jnp.int32)[:, None] + slots[None, :]
    valid = slots[None, :] < child_len.astype(jnp.int32)[:, None]
    index = jnp.clip(index, 0, PIVOTS - 1).reshape(-1)
    picked = jnp.take(solution, index, axis=1)
    return jnp.where(valid.reshape(-1)[None, :], picked, jnp.zeros_like(picked))
```

```python
import jax
import jax.numpy as jnp
from jax import lax
from jax.experimental import pallas as pl
from jax.experimental.pallas import tpu as pltpu
from jax.sharding import Mesh
from jax.sharding import PartitionSpec as P

BLK = 128
ROWS = ("z", "x")
PIV = ("y", "c")
VMEM = pl.BlockSpec(memory_space=pltpu.VMEM)
SMEM = pl.BlockSpec(memory_space=pltpu.SMEM)


def exchange(value, axes):
    return lax.all_to_all(value, axes, split_axis=0, concat_axis=0, tiled=True)


def spread(value, axis):
    count = lax.axis_size(axis)
    return exchange(jnp.broadcast_to(value[None], (count, *value.shape)), axis)


def pack_kernel(count, maps, column, sends):
    across = maps.shape[0]
    for dest in range(across):
        for slot in range(count):
            block = maps[dest, slot]
            level = lax.div(block, count * across)
            offset = pl.multiple_of(lax.rem(block, count) * BLK, BLK)
            sends[dest, :, slot * BLK : (slot + 1) * BLK] = column[level, :, pl.ds(offset, BLK)]


def pick_kernel(count, own, arrived, boundary):
    across = arrived.shape[0]
    for slot in range(count):
        origin = lax.rem(lax.div(own[slot], count), across)
        cols = slice(slot * BLK, (slot + 1) * BLK)
        boundary[:, cols] = arrived[origin, :, cols]


def child_kernel(first, length, pieces, children, summed):
    quarters, _, rows, span = pieces.shape
    padded = summed.shape[1]
    for quarter in range(quarters):
        own = slice(quarter * rows, (quarter + 1) * rows)
        summed[own, :span] = jnp.sum(pieces[quarter], axis=0)
    summed[:, span:] = jnp.zeros((quarters * rows, padded - span), jnp.float32)
    lane = lax.broadcasted_iota(jnp.int32, (quarters * rows, BLK), 1)
    for child in range(first.shape[0]):
        offset = jnp.clip(first[child], 0, span - 1)
        tile = lax.div(offset, BLK)
        window = summed[:, pl.ds(pl.multiple_of(tile * BLK, BLK), 2 * BLK)]
        shift = lax.rem(2 * BLK - (offset - tile * BLK), 2 * BLK)
        moved = pltpu.roll(window, shift, 1)[:, :BLK]
        children[:, child * BLK : (child + 1) * BLK] = jnp.where(
            lane < length[child], moved, jnp.zeros_like(moved)
        )


def body(ancestor_sol, front_map, lower_panel, inverse_factor, right_side, child_start, child_len):
    deep, across, tall, cores = (lax.axis_size(a) for a in ("z", "x", "y", "c"))
    srcs, width = ancestor_sol.shape
    count = front_map.shape[0]
    pivots, span = inverse_factor.shape
    total = right_side.shape[0]
    piv_devs = tall * cores
    part = srcs // across
    quarter = total // across
    me = lax.axis_index(ROWS)

    maps = spread(front_map, "x").reshape(across, count)
    column = lax.all_gather(ancestor_sol, "z", axis=0, tiled=False)
    half = pivots // 2
    inverse_lo = spread(inverse_factor[:half], "x")
    own_share = right_side.shape[1]
    place = (
        jnp.arange(pivots, dtype=jnp.int32)[None, :]
        == me * own_share + jnp.arange(own_share, dtype=jnp.int32)[:, None]
    ).astype(jnp.float32)
    ordered = right_side.reshape(piv_devs, across, part, own_share).swapaxes(0, 1)
    placed = jnp.dot(
        ordered.reshape(total, own_share),
        place,
        precision=lax.Precision.HIGHEST,
        preferred_element_type=jnp.float32,
    )
    column, inverse_lo, maps, placed = lax.optimization_barrier((column, inverse_lo, maps, placed))
    sends = pl.pallas_call(
        lambda *refs: pack_kernel(count, *refs),
        out_shape=jax.ShapeDtypeStruct((across, srcs, width), jnp.float32),
        in_specs=[SMEM, VMEM],
        out_specs=VMEM,
        name="pack",
    )(maps, column)
    arrived = exchange(sends, "x")
    boundary = pl.pallas_call(
        lambda *refs: pick_kernel(count, *refs),
        out_shape=jax.ShapeDtypeStruct((srcs, width), jnp.float32),
        in_specs=[SMEM, VMEM],
        out_specs=VMEM,
        name="pick",
    )(front_map, arrived)
    boundary, upper = lax.optimization_barrier((boundary, inverse_factor[half:]))
    inverse_hi = spread(upper, "x")
    full = lax.all_gather(boundary.reshape(across, part, width), PIV, axis=1, tiled=True)
    full, inverse_hi = lax.optimization_barrier((full, inverse_hi))
    share = placed - jnp.dot(
        full.reshape(total, width),
        lower_panel,
        precision=lax.Precision.HIGH,
        preferred_element_type=jnp.float32,
    )
    reduced = exchange(share.reshape(across, quarter, pivots), "x").sum(axis=0)
    reduced = exchange(reduced.reshape(deep, quarter // deep, pivots), "z").sum(axis=0)
    reduced = spread(reduced, "z").reshape(quarter, pivots)
    inverse = jnp.concatenate(
        [inverse_lo.reshape(across, half, span), inverse_hi.reshape(across, half, span)], axis=1
    )
    partial = jnp.stack(
        [
            jnp.dot(
                reduced,
                inverse[group],
                precision=lax.Precision.HIGH,
                preferred_element_type=jnp.float32,
            )
            for group in range(across)
        ]
    )
    partial = partial.reshape(across, tall, cores, part, span)
    core = lax.axis_index("c")
    kept = lax.dynamic_index_in_dim(partial, core, 2, keepdims=False)
    other = lax.dynamic_index_in_dim(partial, 1 - core, 2, keepdims=False)
    kept = kept + lax.ppermute(other, "c", [(0, 1), (1, 0)])
    pieces = exchange(kept.reshape(across * tall, part, span), ("x", "y"))
    return pl.pallas_call(
        child_kernel,
        out_shape=jax.ShapeDtypeStruct((srcs, child_len.shape[0] * BLK), jnp.float32),
        in_specs=[SMEM, SMEM, VMEM],
        out_specs=VMEM,
        scratch_shapes=[pltpu.VMEM((srcs, span + BLK), jnp.float32)],
        name="children",
    )(child_start - me * span, child_len, pieces.reshape(across, tall, part, span))


def solution(mesh):
    piv = mesh.shape["piv"]
    torus = Mesh(mesh.devices.reshape(8, 4, piv // 2, 2), ("z", "x", "y", "c"))
    return jax.shard_map(
        body,
        mesh=torus,
        in_specs=(
            P(PIV, ROWS),
            P(ROWS),
            P(ROWS, PIV),
            P(PIV, ROWS),
            P(None, PIV + ROWS),
            P(ROWS),
            P(ROWS),
        ),
        out_specs=P(PIV, ROWS),
        check_vma=False,
    )
```

```python
import jax
import jax.numpy as jnp
from jax import lax
from jax.experimental import pallas as pl
from jax.experimental.pallas import tpu as pltpu
from jax.sharding import Mesh
from jax.sharding import PartitionSpec as P

BLK = 128
ROWS = ("z", "x")
PIV = ("y", "c")
VMEM = pl.BlockSpec(memory_space=pltpu.VMEM)
SMEM = pl.BlockSpec(memory_space=pltpu.SMEM)


def exchange(value, axes):
    return lax.all_to_all(value, axes, split_axis=0, concat_axis=0, tiled=True)


def spread(value, axis):
    count = lax.axis_size(axis)
    return exchange(jnp.broadcast_to(value[None], (count, *value.shape)), axis)


def pack_kernel(count, maps, column, sends):
    across = maps.shape[0]
    for dest in range(across):
        for slot in range(count):
            block = maps[dest, slot]
            level = lax.div(block, count * across)
            offset = pl.multiple_of(lax.rem(block, count) * BLK, BLK)
            sends[dest, :, slot * BLK : (slot + 1) * BLK] = column[level, :, pl.ds(offset, BLK)]


def pick_kernel(count, own, arrived, boundary):
    across = arrived.shape[0]
    for slot in range(count):
        origin = lax.rem(lax.div(own[slot], count), across)
        cols = slice(slot * BLK, (slot + 1) * BLK)
        boundary[:, cols] = arrived[origin, :, cols]


def split(value):
    high = value.astype(jnp.bfloat16)
    return high, (value - high.astype(jnp.float32)).astype(jnp.bfloat16)


def product(left, right):
    terms = ((0, 0), (0, 1), (1, 0))
    return sum(jnp.dot(left[i], right[j], preferred_element_type=jnp.float32) for i, j in terms)


def couple_kernel(full, panel, placed, share_a, share_b, high, low):
    @pl.when(pl.program_id(0) == 0)
    def _():
        high[...], low[...] = split(panel[...])

    _, devs, part, width = full.shape
    short = part // 2
    pivots = panel.shape[1]
    left = split(full[0].reshape(devs * part, width))
    result = placed[0].reshape(devs * part, pivots) - product(left, (high[...], low[...]))
    result = result.reshape(devs, 2, short, pivots)
    share_a[0] = result[:, 0].reshape(share_a.shape[1:])
    share_b[:, 0] = result[:, 1].reshape(share_b.shape[0], *share_b.shape[2:])


def join_kernel(pieces_a, pieces_b, copies):
    joined = (jnp.sum(pieces_a[...], axis=0), jnp.sum(pieces_b[...], axis=0))
    for level in range(copies.shape[0]):
        for side in range(2):
            copies[level, side] = joined[side]


def solve_kernel(core, reduced, inverse_lo, inverse_hi, kept, other, high, low):
    @pl.when(pl.program_id(0) == 0)
    def _():
        high[...], low[...] = split(reduced[...])

    _, tall, halves, short, span = kept.shape
    half = inverse_lo.shape[1]
    result = product((high[:, :half], low[:, :half]), split(inverse_lo[0]))
    result = result + product((high[:, half:], low[:, half:]), split(inverse_hi[0]))
    result = result.reshape(tall, halves, 2, short, span)
    first, second = result[:, :, 0], result[:, :, 1]
    mine = core[0] == 0
    kept[0] = jnp.where(mine, first, second)
    other[0] = jnp.where(mine, second, first)


def child_kernel(first, length, pieces, children, summed):
    quarters, _, rows, span = pieces.shape
    padded = summed.shape[1]
    for quarter in range(quarters):
        own = slice(quarter * rows, (quarter + 1) * rows)
        summed[own, :span] = jnp.sum(pieces[quarter], axis=0)
    summed[:, span:] = jnp.zeros((quarters * rows, padded - span), jnp.float32)
    lane = lax.broadcasted_iota(jnp.int32, (quarters * rows, BLK), 1)
    for child in range(first.shape[0]):
        offset = jnp.clip(first[child], 0, span - 1)
        tile = lax.div(offset, BLK)
        window = summed[:, pl.ds(pl.multiple_of(tile * BLK, BLK), 2 * BLK)]
        shift = lax.rem(2 * BLK - (offset - tile * BLK), 2 * BLK)
        moved = pltpu.roll(window, shift, 1)[:, :BLK]
        children[:, child * BLK : (child + 1) * BLK] = jnp.where(
            lane < length[child], moved, jnp.zeros_like(moved)
        )


def body(ancestor_sol, front_map, lower_panel, inverse_factor, right_side, child_start, child_len):
    deep, across, tall, cores = (lax.axis_size(a) for a in ("z", "x", "y", "c"))
    srcs, width = ancestor_sol.shape
    count = front_map.shape[0]
    pivots, span = inverse_factor.shape
    total = right_side.shape[0]
    piv_devs = tall * cores
    part = srcs // across
    quarter = total // across
    me = lax.axis_index(ROWS)

    maps = spread(front_map, "x").reshape(across, count)
    column = lax.all_gather(ancestor_sol, "z", axis=0, tiled=False)
    half = pivots // 2
    inverse_lo = spread(inverse_factor[:half], "x")
    column, inverse_lo, maps = lax.optimization_barrier((column, inverse_lo, maps))
    sends = pl.pallas_call(
        lambda *refs: pack_kernel(count, *refs),
        out_shape=jax.ShapeDtypeStruct((across, srcs, width), jnp.float32),
        in_specs=[SMEM, VMEM],
        out_specs=VMEM,
        name="pack",
    )(maps, column)
    arrived = exchange(sends, "x")
    boundary = pl.pallas_call(
        lambda *refs: pick_kernel(count, *refs),
        out_shape=jax.ShapeDtypeStruct((srcs, width), jnp.float32),
        in_specs=[SMEM, VMEM],
        out_specs=VMEM,
        name="pick",
    )(front_map, arrived)
    boundary, upper, right_side = lax.optimization_barrier(
        (boundary, inverse_factor[half:], right_side)
    )
    inverse_hi = spread(upper, "x")
    own_share = right_side.shape[1]
    place = (
        jnp.arange(pivots, dtype=jnp.int32)[None, :]
        == me * own_share + jnp.arange(own_share, dtype=jnp.int32)[:, None]
    ).astype(jnp.float32)
    ordered = right_side.reshape(piv_devs, across, part, own_share).swapaxes(0, 1)
    placed = jnp.dot(
        ordered.reshape(total, own_share),
        place,
        precision=lax.Precision.HIGHEST,
        preferred_element_type=jnp.float32,
    ).reshape(across, piv_devs, part, pivots)
    full = lax.all_gather(boundary.reshape(across, part, width), PIV, axis=1, tiled=True)
    full, inverse_hi, placed = lax.optimization_barrier((full, inverse_hi, placed))
    short = part // 2
    rows = piv_devs * short
    chip = cores * short
    share_a, share_b = pl.pallas_call(
        couple_kernel,
        grid=(across,),
        out_shape=(
            jax.ShapeDtypeStruct((across, rows, pivots), jnp.float32),
            jax.ShapeDtypeStruct((tall, across, chip, pivots), jnp.float32),
        ),
        in_specs=[
            pl.BlockSpec((1, piv_devs, part, width), lambda i: (i, 0, 0, 0)),
            pl.BlockSpec((width, pivots), lambda i: (0, 0)),
            pl.BlockSpec((1, piv_devs, part, pivots), lambda i: (i, 0, 0, 0)),
        ],
        out_specs=(
            pl.BlockSpec((1, rows, pivots), lambda i: (i, 0, 0)),
            pl.BlockSpec((tall, 1, chip, pivots), lambda i: (0, i, 0, 0)),
        ),
        scratch_shapes=[
            pltpu.VMEM((width, pivots), jnp.bfloat16),
            pltpu.VMEM((width, pivots), jnp.bfloat16),
        ],
        compiler_params=pltpu.CompilerParams(vmem_limit_bytes=48 * 1024 * 1024),
        name="couple",
    )(full.reshape(across, piv_devs, part, width), lower_panel, placed)
    nearer_b = lax.psum_scatter(share_b, "z", scatter_dimension=0, tiled=True)
    nearer_a = exchange(share_a, "x").sum(axis=0)
    nearer_a = exchange(nearer_a.reshape(deep, chip, pivots), "z")
    nearer_a, nearer_b = lax.optimization_barrier((nearer_a, nearer_b))
    nearer_b = exchange(nearer_b.reshape(across, chip, pivots), "x")
    copies = pl.pallas_call(
        join_kernel,
        out_shape=jax.ShapeDtypeStruct((deep, 2, chip, pivots), jnp.float32),
        in_specs=[VMEM, VMEM],
        out_specs=VMEM,
        name="join",
    )(nearer_a, nearer_b)
    reduced = exchange(copies, "z").reshape(quarter, pivots)
    core = lax.axis_index("c")
    kept, other = pl.pallas_call(
        solve_kernel,
        grid=(across,),
        out_shape=(jax.ShapeDtypeStruct((across, tall, 2, short, span), jnp.float32),) * 2,
        in_specs=[
            SMEM,
            pl.BlockSpec((quarter, pivots), lambda i: (0, 0)),
            pl.BlockSpec((1, half, span), lambda i: (i, 0, 0)),
            pl.BlockSpec((1, half, span), lambda i: (i, 0, 0)),
        ],
        out_specs=(pl.BlockSpec((1, tall, 2, short, span), lambda i: (i, 0, 0, 0, 0)),) * 2,
        scratch_shapes=[
            pltpu.VMEM((quarter, pivots), jnp.bfloat16),
            pltpu.VMEM((quarter, pivots), jnp.bfloat16),
        ],
        name="solve",
    )(
        core.reshape(1),
        reduced,
        inverse_lo.reshape(across, half, span),
        inverse_hi.reshape(across, half, span),
    )
    kept = kept + lax.ppermute(other, "c", [(0, 1), (1, 0)])
    pieces = exchange(kept.reshape(across * tall, part, span), ("x", "y"))
    return pl.pallas_call(
        child_kernel,
        out_shape=jax.ShapeDtypeStruct((srcs, child_len.shape[0] * BLK), jnp.float32),
        in_specs=[SMEM, SMEM, VMEM],
        out_specs=VMEM,
        scratch_shapes=[pltpu.VMEM((srcs, span + BLK), jnp.float32)],
        name="children",
    )(child_start - me * span, child_len, pieces.reshape(across, tall, part, span))


def solution(mesh):
    piv = mesh.shape["piv"]
    torus = Mesh(mesh.devices.reshape(8, 4, piv // 2, 2), ("z", "x", "y", "c"))
    return jax.shard_map(
        body,
        mesh=torus,
        in_specs=(
            P(PIV, ROWS),
            P(ROWS),
            P(ROWS, PIV),
            P(PIV, ROWS),
            P(None, PIV + ROWS),
            P(ROWS),
            P(ROWS),
        ),
        out_specs=P(PIV, ROWS),
        check_vma=False,
    )
```

```python
import jax
import jax.numpy as jnp
from jax import lax
from jax.experimental import pallas as pl
from jax.experimental.pallas import tpu as pltpu
from jax.sharding import Mesh
from jax.sharding import PartitionSpec as P

BLK = 128
ROWS = ("z", "x")
PIV = ("y", "c")
VMEM = pl.BlockSpec(memory_space=pltpu.VMEM)
SMEM = pl.BlockSpec(memory_space=pltpu.SMEM)


def grant(size):
    return pltpu.CompilerParams(vmem_limit_bytes=size << 20)


def exchange(value, axes):
    return lax.all_to_all(value, axes, split_axis=0, concat_axis=0, tiled=True)


def spread(value, axis):
    count = lax.axis_size(axis)
    return exchange(jnp.broadcast_to(value[None], (count, *value.shape)), axis)


def pack_kernel(count, maps, column, sends):
    across = maps.shape[0]
    for dest in range(across):
        for slot in range(count):
            block = maps[dest, slot]
            level = lax.div(block, count * across)
            offset = pl.multiple_of(lax.rem(block, count) * BLK, BLK)
            sends[dest, :, slot * BLK : (slot + 1) * BLK] = column[level, :, pl.ds(offset, BLK)]


def pick_kernel(count, own, arrived, boundary):
    across = arrived.shape[0]
    for slot in range(count):
        origin = lax.rem(lax.div(own[slot], count), across)
        cols = slice(slot * BLK, (slot + 1) * BLK)
        boundary[:, cols] = arrived[origin, :, cols]


def split(value):
    high = value.astype(jnp.bfloat16)
    return high, (value - high.astype(jnp.float32)).astype(jnp.bfloat16)


def product(left, right):
    terms = ((0, 0), (0, 1), (1, 0))
    return sum(jnp.dot(left[i], right[j], preferred_element_type=jnp.float32) for i, j in terms)


def halve_kernel(value, high, low):
    high[...], low[...] = split(value[...])


def halve_inverse_kernel(inverse_lo, inverse_hi, high, low):
    half = inverse_lo.shape[1]
    high[:, :half], low[:, :half] = split(inverse_lo[...])
    high[:, half:], low[:, half:] = split(inverse_hi[...])


def couple_kernel(full, high, low, placed, share_a, share_b):
    left = split(full[0])
    result = placed[0] - product(left, (high[...], low[...]))
    cut = share_a.shape[2]
    share_a[0] = result[:, :cut]
    share_b[:, 0] = result[:, cut:].reshape(share_b.shape[0], *share_b.shape[2:])


def join_kernel(pieces_a, pieces_b, copies):
    first, second = jnp.sum(pieces_a[...], axis=0), jnp.sum(pieces_b[...], axis=0)
    cut = first.shape[1]
    for level in range(copies.shape[0]):
        copies[level, :, :cut] = first
        copies[level, :, cut:] = second


def solve_kernel(core, reduced, inverse_high, inverse_low, kept, other, high, low):
    @pl.when(pl.program_id(0) == 0)
    def _():
        high[...], low[...] = split(reduced[...])

    _, tall, part, span = kept.shape
    result = product((high[...], low[...]), (inverse_high[0], inverse_low[0]))
    result = result.reshape(tall, 2, part, span)
    first, second = result[:, 0], result[:, 1]
    mine = core[0] == 0
    kept[0] = jnp.where(mine, first, second)
    other[0] = jnp.where(mine, second, first)


def child_kernel(first, length, pieces, children, summed):
    quarters, _, rows, span = pieces.shape
    padded = summed.shape[1]
    for quarter in range(quarters):
        own = slice(quarter * rows, (quarter + 1) * rows)
        summed[own, :span] = jnp.sum(pieces[quarter], axis=0)
    summed[:, span:] = jnp.zeros((quarters * rows, padded - span), jnp.float32)
    lane = lax.broadcasted_iota(jnp.int32, (quarters * rows, BLK), 1)
    for child in range(first.shape[0]):
        offset = jnp.clip(first[child], 0, span - 1)
        tile = lax.div(offset, BLK)
        window = summed[:, pl.ds(pl.multiple_of(tile * BLK, BLK), 2 * BLK)]
        shift = lax.rem(2 * BLK - (offset - tile * BLK), 2 * BLK)
        moved = pltpu.roll(window, shift, 1)[:, :BLK]
        children[:, child * BLK : (child + 1) * BLK] = jnp.where(
            lane < length[child], moved, jnp.zeros_like(moved)
        )


def body(ancestor_sol, front_map, lower_panel, inverse_factor, right_side, child_start, child_len):
    deep, across, tall, cores = (lax.axis_size(a) for a in ("z", "x", "y", "c"))
    srcs, width = ancestor_sol.shape
    count = front_map.shape[0]
    pivots, span = inverse_factor.shape
    total = right_side.shape[0]
    piv_devs = tall * cores
    part = srcs // across
    quarter = total // across
    me = lax.axis_index(ROWS)

    core = lax.axis_index("c").reshape(1)
    first = child_start - me * span
    maps = spread(front_map, "x").reshape(across, count)
    column = lax.all_gather(ancestor_sol, "z", axis=0, tiled=False)
    half = pivots // 2
    inverse_lo = spread(inverse_factor[:half], "x")
    panel_high, panel_low = pl.pallas_call(
        halve_kernel,
        grid=(4,),
        out_shape=(jax.ShapeDtypeStruct((width, pivots), jnp.bfloat16),) * 2,
        in_specs=[pl.BlockSpec((width // 4, pivots), lambda i: (i, 0))],
        out_specs=(pl.BlockSpec((width // 4, pivots), lambda i: (i, 0)),) * 2,
        compiler_params=grant(60),
        name="halve",
    )(lower_panel)
    column, inverse_lo, maps, panel_high, panel_low, core, first = lax.optimization_barrier(
        (column, inverse_lo, maps, panel_high, panel_low, core, first)
    )
    sends = pl.pallas_call(
        lambda *refs: pack_kernel(count, *refs),
        out_shape=jax.ShapeDtypeStruct((across, srcs, width), jnp.float32),
        in_specs=[SMEM, VMEM],
        out_specs=VMEM,
        compiler_params=grant(12),
        name="pack",
    )(maps, column)
    arrived = exchange(sends, "x")
    boundary = pl.pallas_call(
        lambda *refs: pick_kernel(count, *refs),
        out_shape=jax.ShapeDtypeStruct((srcs, width), jnp.float32),
        in_specs=[SMEM, VMEM],
        out_specs=VMEM,
        compiler_params=grant(8),
        name="pick",
    )(front_map, arrived)
    boundary, upper, right_side = lax.optimization_barrier(
        (boundary, inverse_factor[half:], right_side)
    )
    inverse_hi = spread(upper, "x")
    own_share = right_side.shape[1]
    place = (
        jnp.arange(pivots, dtype=jnp.int32)[None, :]
        == me * own_share + jnp.arange(own_share, dtype=jnp.int32)[:, None]
    ).astype(jnp.float32)
    ordered = right_side.reshape(piv_devs, across, part, own_share).swapaxes(0, 1)
    placed = jnp.dot(
        ordered.reshape(total, own_share),
        place,
        precision=lax.Precision.HIGHEST,
        preferred_element_type=jnp.float32,
    ).reshape(across, quarter, pivots)
    inverse_high, inverse_low = pl.pallas_call(
        halve_inverse_kernel,
        grid=(across,),
        out_shape=(jax.ShapeDtypeStruct((across, pivots, span), jnp.bfloat16),) * 2,
        in_specs=[pl.BlockSpec((1, half, span), lambda i: (i, 0, 0))] * 2,
        out_specs=(pl.BlockSpec((1, pivots, span), lambda i: (i, 0, 0)),) * 2,
        compiler_params=grant(60),
        name="halve_inverse",
    )(inverse_lo.reshape(across, half, span), inverse_hi.reshape(across, half, span))
    full = lax.all_gather(boundary.reshape(across, part, width), PIV, axis=1, tiled=True)
    full, inverse_high, inverse_low, placed = lax.optimization_barrier(
        (full, inverse_high, inverse_low, placed)
    )
    cut = pivots // 3 * 2
    rest = pivots - cut
    few = quarter // deep
    share_a, share_b = pl.pallas_call(
        couple_kernel,
        grid=(across,),
        out_shape=(
            jax.ShapeDtypeStruct((across, quarter, cut), jnp.float32),
            jax.ShapeDtypeStruct((deep, across, few, rest), jnp.float32),
        ),
        in_specs=[
            pl.BlockSpec((1, quarter, width), lambda i: (i, 0, 0)),
            pl.BlockSpec((width, pivots), lambda i: (0, 0)),
            pl.BlockSpec((width, pivots), lambda i: (0, 0)),
            pl.BlockSpec((1, quarter, pivots), lambda i: (i, 0, 0)),
        ],
        out_specs=(
            pl.BlockSpec((1, quarter, cut), lambda i: (i, 0, 0)),
            pl.BlockSpec((deep, 1, few, rest), lambda i: (0, i, 0, 0)),
        ),
        compiler_params=grant(60),
        name="couple",
    )(full, panel_high, panel_low, placed)
    nearer_b = lax.psum_scatter(share_b, "z", scatter_dimension=0, tiled=True)
    nearer_a = exchange(share_a, "x").sum(axis=0)
    nearer_a = exchange(nearer_a.reshape(deep, few, cut), "z")
    nearer_a, nearer_b = lax.optimization_barrier((nearer_a, nearer_b))
    nearer_b = exchange(nearer_b.reshape(across, few, rest), "x")
    copies = pl.pallas_call(
        join_kernel,
        out_shape=jax.ShapeDtypeStruct((deep, few, pivots), jnp.float32),
        in_specs=[VMEM, VMEM],
        out_specs=VMEM,
        compiler_params=grant(8),
        name="join",
    )(nearer_a, nearer_b)
    reduced = exchange(copies, "z").reshape(quarter, pivots)
    kept, other = pl.pallas_call(
        solve_kernel,
        grid=(across,),
        out_shape=(jax.ShapeDtypeStruct((across, tall, part, span), jnp.float32),) * 2,
        in_specs=[
            SMEM,
            pl.BlockSpec((quarter, pivots), lambda i: (0, 0)),
            pl.BlockSpec((1, pivots, span), lambda i: (i, 0, 0)),
            pl.BlockSpec((1, pivots, span), lambda i: (i, 0, 0)),
        ],
        out_specs=(pl.BlockSpec((1, tall, part, span), lambda i: (i, 0, 0, 0)),) * 2,
        scratch_shapes=[
            pltpu.VMEM((quarter, pivots), jnp.bfloat16),
            pltpu.VMEM((quarter, pivots), jnp.bfloat16),
        ],
        compiler_params=grant(60),
        name="solve",
    )(core, reduced, inverse_high, inverse_low)
    kept = kept + lax.ppermute(other, "c", [(0, 1), (1, 0)])
    pieces = exchange(kept.reshape(across * tall, part, span), ("x", "y"))
    return pl.pallas_call(
        child_kernel,
        out_shape=jax.ShapeDtypeStruct((srcs, child_len.shape[0] * BLK), jnp.float32),
        in_specs=[SMEM, SMEM, VMEM],
        out_specs=VMEM,
        scratch_shapes=[pltpu.VMEM((srcs, span + BLK), jnp.float32)],
        compiler_params=grant(8),
        name="children",
    )(first, child_len, pieces.reshape(across, tall, part, span))


def solution(mesh):
    piv = mesh.shape["piv"]
    torus = Mesh(mesh.devices.reshape(8, 4, piv // 2, 2), ("z", "x", "y", "c"))
    return jax.shard_map(
        body,
        mesh=torus,
        in_specs=(
            P(PIV, ROWS),
            P(ROWS),
            P(ROWS, PIV),
            P(PIV, ROWS),
            P(None, PIV + ROWS),
            P(ROWS),
            P(ROWS),
        ),
        out_specs=P(PIV, ROWS),
        check_vma=False,
    )
```

```python
import jax
import jax.numpy as jnp
from jax import lax
from jax.experimental import pallas as pl
from jax.experimental.pallas import tpu as pltpu
from jax.sharding import Mesh
from jax.sharding import PartitionSpec as P

BLK = 128
ROWS = ("z", "x")
PIV = ("y", "c")
VMEM = pl.BlockSpec(memory_space=pltpu.VMEM)
SMEM = pl.BlockSpec(memory_space=pltpu.SMEM)


def grant(size):
    return pltpu.CompilerParams(vmem_limit_bytes=size << 20)


def exchange(value, axes):
    return lax.all_to_all(value, axes, split_axis=0, concat_axis=0, tiled=True)


def spread(value, axis):
    count = lax.axis_size(axis)
    return exchange(jnp.broadcast_to(value[None], (count, *value.shape)), axis)


def pack_kernel(count, maps, column, sends):
    across = maps.shape[0]
    for dest in range(across):
        for slot in range(count):
            block = maps[dest, slot]
            level = lax.div(block, count * across)
            offset = pl.multiple_of(lax.rem(block, count) * BLK, BLK)
            sends[dest, :, slot * BLK : (slot + 1) * BLK] = column[level, :, pl.ds(offset, BLK)]


def pick_kernel(count, own, arrived, boundary):
    across = arrived.shape[0]
    for slot in range(count):
        origin = lax.rem(lax.div(own[slot], count), across)
        cols = slice(slot * BLK, (slot + 1) * BLK)
        boundary[:, cols] = arrived[origin, :, cols]


def split(value):
    high = value.astype(jnp.bfloat16)
    return high, (value - high.astype(jnp.float32)).astype(jnp.bfloat16)


def product(left, right):
    terms = ((0, 0), (0, 1), (1, 0))
    return sum(jnp.dot(left[i], right[j], preferred_element_type=jnp.float32) for i, j in terms)


def halve_kernel(value, high, low):
    high[...], low[...] = split(value[...])


def halve_inverse_kernel(inverse_lo, inverse_hi, high, low):
    half = inverse_lo.shape[1]
    high[:, :half], low[:, :half] = split(inverse_lo[...])
    high[:, half:], low[:, half:] = split(inverse_hi[...])


def couple_kernel(position, full, high, low, placed, *shares):
    across = len(shares)
    step = pl.program_id(0)
    result = placed[0] - product(split(full[0]), (high[...], low[...]))
    for slot in range(across):

        @pl.when(step == (slot + across - 1) % across)
        def _():
            shares[slot][...] = result


def join_kernel(pieces_a, pieces_b, copies):
    first, second = jnp.sum(pieces_a[...], axis=0), jnp.sum(pieces_b[...], axis=0)
    cut = first.shape[1]
    for level in range(copies.shape[0]):
        copies[level, :, :cut] = first
        copies[level, :, cut:] = second


def solve_kernel(core, reduced, inverse_high, inverse_low, kept, other, high, low):
    @pl.when(pl.program_id(0) == 0)
    def _():
        high[...], low[...] = split(reduced[...])

    _, tall, part, span = kept.shape
    result = product((high[...], low[...]), (inverse_high[0], inverse_low[0]))
    result = result.reshape(tall, 2, part, span)
    first, second = result[:, 0], result[:, 1]
    mine = core[0] == 0
    kept[0] = jnp.where(mine, first, second)
    other[0] = jnp.where(mine, second, first)


def child_kernel(first, length, pieces, children, summed):
    quarters, _, rows, span = pieces.shape
    padded = summed.shape[1]
    for quarter in range(quarters):
        own = slice(quarter * rows, (quarter + 1) * rows)
        summed[own, :span] = jnp.sum(pieces[quarter], axis=0)
    summed[:, span:] = jnp.zeros((quarters * rows, padded - span), jnp.float32)
    lane = lax.broadcasted_iota(jnp.int32, (quarters * rows, BLK), 1)
    for child in range(first.shape[0]):
        offset = jnp.clip(first[child], 0, span - 1)
        tile = lax.div(offset, BLK)
        window = summed[:, pl.ds(pl.multiple_of(tile * BLK, BLK), 2 * BLK)]
        shift = lax.rem(2 * BLK - (offset - tile * BLK), 2 * BLK)
        moved = pltpu.roll(window, shift, 1)[:, :BLK]
        children[:, child * BLK : (child + 1) * BLK] = jnp.where(
            lane < length[child], moved, jnp.zeros_like(moved)
        )


def body(ancestor_sol, front_map, lower_panel, inverse_factor, right_side, child_start, child_len):
    deep, across, tall, cores = (lax.axis_size(a) for a in ("z", "x", "y", "c"))
    srcs, width = ancestor_sol.shape
    count = front_map.shape[0]
    pivots, span = inverse_factor.shape
    total = right_side.shape[0]
    piv_devs = tall * cores
    part = srcs // across
    quarter = total // across
    me = lax.axis_index(ROWS)

    core = lax.axis_index("c").reshape(1)
    first = child_start - me * span
    maps = spread(front_map, "x").reshape(across, count)
    column = lax.all_gather(ancestor_sol, "z", axis=0, tiled=False)
    half = pivots // 2
    inverse_lo = spread(inverse_factor[:half], "x")
    panel_high, panel_low = pl.pallas_call(
        halve_kernel,
        grid=(4,),
        out_shape=(jax.ShapeDtypeStruct((width, pivots), jnp.bfloat16),) * 2,
        in_specs=[pl.BlockSpec((width // 4, pivots), lambda i: (i, 0))],
        out_specs=(pl.BlockSpec((width // 4, pivots), lambda i: (i, 0)),) * 2,
        compiler_params=grant(60),
        name="halve",
    )(lower_panel)
    column, inverse_lo, maps, panel_high, panel_low, core, first = lax.optimization_barrier(
        (column, inverse_lo, maps, panel_high, panel_low, core, first)
    )
    sends = pl.pallas_call(
        lambda *refs: pack_kernel(count, *refs),
        out_shape=jax.ShapeDtypeStruct((across, srcs, width), jnp.float32),
        in_specs=[SMEM, VMEM],
        out_specs=VMEM,
        compiler_params=grant(12),
        name="pack",
    )(maps, column)
    arrived = exchange(sends, "x")
    boundary = pl.pallas_call(
        lambda *refs: pick_kernel(count, *refs),
        out_shape=jax.ShapeDtypeStruct((srcs, width), jnp.float32),
        in_specs=[SMEM, VMEM],
        out_specs=VMEM,
        compiler_params=grant(8),
        name="pick",
    )(front_map, arrived)
    boundary, upper, right_side = lax.optimization_barrier(
        (boundary, inverse_factor[half:], right_side)
    )
    inverse_hi = spread(upper, "x")
    own_share = right_side.shape[1]
    place = (
        jnp.arange(pivots, dtype=jnp.int32)[None, :]
        == me * own_share + jnp.arange(own_share, dtype=jnp.int32)[:, None]
    ).astype(jnp.float32)
    ordered = right_side.reshape(piv_devs, across, part, own_share).swapaxes(0, 1)
    placed = jnp.dot(
        ordered.reshape(total, own_share),
        place,
        precision=lax.Precision.HIGHEST,
        preferred_element_type=jnp.float32,
    ).reshape(across, quarter, pivots)
    inverse_high, inverse_low = pl.pallas_call(
        halve_inverse_kernel,
        grid=(across,),
        out_shape=(jax.ShapeDtypeStruct((across, pivots, span), jnp.bfloat16),) * 2,
        in_specs=[pl.BlockSpec((1, half, span), lambda i: (i, 0, 0))] * 2,
        out_specs=(pl.BlockSpec((1, pivots, span), lambda i: (i, 0, 0)),) * 2,
        compiler_params=grant(60),
        name="halve_inverse",
    )(inverse_lo.reshape(across, half, span), inverse_hi.reshape(across, half, span))
    full = lax.all_gather(boundary.reshape(across, part, width), PIV, axis=1, tiled=True)
    full, inverse_high, inverse_low, placed = lax.optimization_barrier(
        (full, inverse_high, inverse_low, placed)
    )
    few = quarter // deep
    position = lax.axis_index("x").reshape(1)

    def coupled(side):
        block = pl.BlockSpec((quarter, half), lambda i, at: (0, 0))
        return pl.pallas_call(
            couple_kernel,
            grid_spec=pltpu.PrefetchScalarGridSpec(
                num_scalar_prefetch=1,
                grid=(across,),
                in_specs=[
                    pl.BlockSpec(
                        (1, quarter, width), lambda i, at: (lax.rem(at[0] + 1 + i, across), 0, 0)
                    ),
                    pl.BlockSpec((width, half), lambda i, at: (0, side)),
                    pl.BlockSpec((width, half), lambda i, at: (0, side)),
                    pl.BlockSpec(
                        (1, quarter, half), lambda i, at: (lax.rem(at[0] + 1 + i, across), 0, side)
                    ),
                ],
                out_specs=(block,) * across,
            ),
            out_shape=(jax.ShapeDtypeStruct((quarter, half), jnp.float32),) * across,
            compiler_params=grant(60),
            cost_estimate=pl.CostEstimate(
                flops=6 * total * width * half,
                bytes_accessed=4 * (total * width + width * half + 2 * total * half),
                transcendentals=0,
            ),
            name="couple",
        )(position, full, panel_high, panel_low, placed)

    def across_sent(shares):
        return [
            lax.ppermute(shares[k], "x", [(i, (i + k) % across) for i in range(across)])
            for k in range(1, across)
        ]

    def nearer(shares, arrived):
        summed = shares[0] + sum(arrived[1:], arrived[0])
        return exchange(summed.reshape(deep, few, half), "z")

    shares_a = coupled(0)
    arrived_a = across_sent(shares_a)
    shares_b = coupled(1)
    arrived_b = across_sent(shares_b)
    nearer_a = nearer(shares_a, arrived_a)
    nearer_b = nearer(shares_b, arrived_b)
    copies = pl.pallas_call(
        join_kernel,
        out_shape=jax.ShapeDtypeStruct((deep, few, pivots), jnp.float32),
        in_specs=[VMEM, VMEM],
        out_specs=VMEM,
        compiler_params=grant(8),
        name="join",
    )(nearer_a, nearer_b)
    reduced = exchange(copies, "z").reshape(quarter, pivots)
    kept, other = pl.pallas_call(
        solve_kernel,
        grid=(across,),
        out_shape=(jax.ShapeDtypeStruct((across, tall, part, span), jnp.float32),) * 2,
        in_specs=[
            SMEM,
            pl.BlockSpec((quarter, pivots), lambda i: (0, 0)),
            pl.BlockSpec((1, pivots, span), lambda i: (i, 0, 0)),
            pl.BlockSpec((1, pivots, span), lambda i: (i, 0, 0)),
        ],
        out_specs=(pl.BlockSpec((1, tall, part, span), lambda i: (i, 0, 0, 0)),) * 2,
        scratch_shapes=[
            pltpu.VMEM((quarter, pivots), jnp.bfloat16),
            pltpu.VMEM((quarter, pivots), jnp.bfloat16),
        ],
        compiler_params=grant(60),
        name="solve",
    )(core, reduced, inverse_high, inverse_low)
    kept = kept + lax.ppermute(other, "c", [(0, 1), (1, 0)])
    pieces = exchange(kept.reshape(across * tall, part, span), ("x", "y"))
    return pl.pallas_call(
        child_kernel,
        out_shape=jax.ShapeDtypeStruct((srcs, child_len.shape[0] * BLK), jnp.float32),
        in_specs=[SMEM, SMEM, VMEM],
        out_specs=VMEM,
        scratch_shapes=[pltpu.VMEM((srcs, span + BLK), jnp.float32)],
        compiler_params=grant(8),
        name="children",
    )(first, child_len, pieces.reshape(across, tall, part, span))


def solution(mesh):
    piv = mesh.shape["piv"]
    torus = Mesh(mesh.devices.reshape(8, 4, piv // 2, 2), ("z", "x", "y", "c"))
    return jax.shard_map(
        body,
        mesh=torus,
        in_specs=(
            P(PIV, ROWS),
            P(ROWS),
            P(ROWS, PIV),
            P(PIV, ROWS),
            P(None, PIV + ROWS),
            P(ROWS),
            P(ROWS),
        ),
        out_specs=P(PIV, ROWS),
        check_vma=False,
    )
```

```python
import jax
import jax.numpy as jnp
from jax import lax
from jax.experimental import pallas as pl
from jax.experimental.pallas import tpu as pltpu
from jax.sharding import Mesh
from jax.sharding import PartitionSpec as P

BLK = 128
ROWS = ("z", "x")
PIV = ("y", "c")
VMEM = pl.BlockSpec(memory_space=pltpu.VMEM)
SMEM = pl.BlockSpec(memory_space=pltpu.SMEM)


def grant(size):
    return pltpu.CompilerParams(vmem_limit_bytes=size << 20)


def exchange(value, axes):
    return lax.all_to_all(value, axes, split_axis=0, concat_axis=0, tiled=True)


def spread(value, axis):
    count = lax.axis_size(axis)
    return exchange(jnp.broadcast_to(value[None], (count, *value.shape)), axis)


def pack_kernel(count, maps, column, sends):
    across = maps.shape[0]
    for dest in range(across):
        for slot in range(count):
            block = maps[dest, slot]
            level = lax.div(block, count * across)
            offset = pl.multiple_of(lax.rem(block, count) * BLK, BLK)
            sends[dest, :, slot * BLK : (slot + 1) * BLK] = column[level, :, pl.ds(offset, BLK)]


def pick_kernel(count, own, arrived, boundary):
    across = arrived.shape[0]
    for slot in range(count):
        origin = lax.rem(lax.div(own[slot], count), across)
        cols = slice(slot * BLK, (slot + 1) * BLK)
        boundary[:, cols] = arrived[origin, :, cols]


def split(value):
    high = value.astype(jnp.bfloat16)
    return high, (value - high.astype(jnp.float32)).astype(jnp.bfloat16)


def product(left, right):
    terms = ((0, 0), (0, 1), (1, 0))
    return sum(jnp.dot(left[i], right[j], preferred_element_type=jnp.float32) for i, j in terms)


def halve_kernel(value, high, low):
    high[...], low[...] = split(value[...])


def halve_inverse_kernel(inverse_lo, inverse_hi, high, low):
    half = inverse_lo.shape[1]
    high[:, :half], low[:, :half] = split(inverse_lo[...])
    high[:, half:], low[:, half:] = split(inverse_hi[...])


def couple_kernel(where, full, high, low, placed, *rest):
    shares, total = rest[:-1], rest[-1]
    across = len(shares) // 2
    step = pl.program_id(0)
    wide = placed.shape[2]
    total[...] = -product(split(full[0]), (high[...], low[...]))
    window = pl.ds(pl.multiple_of(where[1] * BLK, BLK), wide)
    total[:, window] = total[:, window] + placed[0]
    half = total.shape[1] // 2
    for slot in range(across):

        @pl.when(step == (slot + across - 1) % across)
        def _():
            shares[slot][...] = total[:, :half]
            shares[across + slot][...] = total[:, half:]


def join_kernel(pieces_a, pieces_b, copies):
    first, second = jnp.sum(pieces_a[...], axis=0), jnp.sum(pieces_b[...], axis=0)
    cut = first.shape[1]
    for level in range(copies.shape[0]):
        copies[level, :, :cut] = first
        copies[level, :, cut:] = second


def solve_kernel(core, reduced, inverse_high, inverse_low, kept, other, high, low):
    @pl.when(pl.program_id(0) == 0)
    def _():
        high[...], low[...] = split(reduced[...])

    _, tall, part, span = kept.shape
    result = product((high[...], low[...]), (inverse_high[0], inverse_low[0]))
    result = result.reshape(tall, 2, part, span)
    first, second = result[:, 0], result[:, 1]
    mine = core[0] == 0
    kept[0] = jnp.where(mine, first, second)
    other[0] = jnp.where(mine, second, first)


def child_kernel(first, length, pieces, children, summed):
    quarters, _, rows, span = pieces.shape
    padded = summed.shape[1]
    for quarter in range(quarters):
        own = slice(quarter * rows, (quarter + 1) * rows)
        summed[own, :span] = jnp.sum(pieces[quarter], axis=0)
    summed[:, span:] = jnp.zeros((quarters * rows, padded - span), jnp.float32)
    lane = lax.broadcasted_iota(jnp.int32, (quarters * rows, BLK), 1)
    for child in range(first.shape[0]):
        offset = jnp.clip(first[child], 0, span - 1)
        tile = lax.div(offset, BLK)
        window = summed[:, pl.ds(pl.multiple_of(tile * BLK, BLK), 2 * BLK)]
        shift = lax.rem(2 * BLK - (offset - tile * BLK), 2 * BLK)
        moved = pltpu.roll(window, shift, 1)[:, :BLK]
        children[:, child * BLK : (child + 1) * BLK] = jnp.where(
            lane < length[child], moved, jnp.zeros_like(moved)
        )


def body(ancestor_sol, front_map, lower_panel, inverse_factor, right_side, child_start, child_len):
    deep, across, tall, cores = (lax.axis_size(a) for a in ("z", "x", "y", "c"))
    srcs, width = ancestor_sol.shape
    count = front_map.shape[0]
    pivots, span = inverse_factor.shape
    total = right_side.shape[0]
    piv_devs = tall * cores
    part = srcs // across
    quarter = total // across
    me = lax.axis_index(ROWS)

    core = lax.axis_index("c").reshape(1)
    first = child_start - me * span
    maps = spread(front_map, "x").reshape(across, count)
    column = lax.all_gather(ancestor_sol, "z", axis=0, tiled=False)
    half = pivots // 2
    inverse_lo = spread(inverse_factor[:half], "x")
    panel_high, panel_low = pl.pallas_call(
        halve_kernel,
        grid=(4,),
        out_shape=(jax.ShapeDtypeStruct((width, pivots), jnp.bfloat16),) * 2,
        in_specs=[pl.BlockSpec((width // 4, pivots), lambda i: (i, 0))],
        out_specs=(pl.BlockSpec((width // 4, pivots), lambda i: (i, 0)),) * 2,
        compiler_params=grant(60),
        name="halve",
    )(lower_panel)
    column, inverse_lo, maps, panel_high, panel_low, core, first = lax.optimization_barrier(
        (column, inverse_lo, maps, panel_high, panel_low, core, first)
    )
    sends = pl.pallas_call(
        lambda *refs: pack_kernel(count, *refs),
        out_shape=jax.ShapeDtypeStruct((across, srcs, width), jnp.float32),
        in_specs=[SMEM, VMEM],
        out_specs=VMEM,
        compiler_params=grant(12),
        name="pack",
    )(maps, column)
    arrived = exchange(sends, "x")
    boundary = pl.pallas_call(
        lambda *refs: pick_kernel(count, *refs),
        out_shape=jax.ShapeDtypeStruct((srcs, width), jnp.float32),
        in_specs=[SMEM, VMEM],
        out_specs=VMEM,
        compiler_params=grant(8),
        name="pick",
    )(front_map, arrived)
    boundary, upper, right_side = lax.optimization_barrier(
        (boundary, inverse_factor[half:], right_side)
    )
    inverse_hi = spread(upper, "x")
    own_share = right_side.shape[1]
    tile = jnp.minimum(lax.div(me * own_share, BLK), pivots // BLK - 2)
    place = (
        jnp.arange(2 * BLK, dtype=jnp.int32)[None, :]
        == me * own_share - tile * BLK + jnp.arange(own_share, dtype=jnp.int32)[:, None]
    ).astype(jnp.float32)
    ordered = right_side.reshape(piv_devs, across, part, own_share).swapaxes(0, 1)
    placed = jnp.dot(
        ordered.reshape(total, own_share),
        place,
        precision=lax.Precision.HIGHEST,
        preferred_element_type=jnp.float32,
    ).reshape(across, quarter, 2 * BLK)
    inverse_high, inverse_low = pl.pallas_call(
        halve_inverse_kernel,
        grid=(across,),
        out_shape=(jax.ShapeDtypeStruct((across, pivots, span), jnp.bfloat16),) * 2,
        in_specs=[pl.BlockSpec((1, half, span), lambda i: (i, 0, 0))] * 2,
        out_specs=(pl.BlockSpec((1, pivots, span), lambda i: (i, 0, 0)),) * 2,
        compiler_params=grant(60),
        name="halve_inverse",
    )(inverse_lo.reshape(across, half, span), inverse_hi.reshape(across, half, span))
    full = lax.all_gather(boundary.reshape(across, part, width), PIV, axis=1, tiled=True)
    full, inverse_high, inverse_low, placed = lax.optimization_barrier(
        (full, inverse_high, inverse_low, placed)
    )
    few = quarter // deep
    where = jnp.stack([lax.axis_index("x"), tile])

    def turn(i, at):
        return (lax.rem(at[0] + 1 + i, across), 0, 0)

    shares = pl.pallas_call(
        couple_kernel,
        grid_spec=pltpu.PrefetchScalarGridSpec(
            num_scalar_prefetch=1,
            grid=(across,),
            in_specs=[
                pl.BlockSpec((1, quarter, width), turn),
                pl.BlockSpec((width, pivots), lambda i, at: (0, 0)),
                pl.BlockSpec((width, pivots), lambda i, at: (0, 0)),
                pl.BlockSpec((1, quarter, 2 * BLK), turn),
            ],
            out_specs=(pl.BlockSpec((quarter, half), lambda i, at: (0, 0)),) * (2 * across),
            scratch_shapes=[pltpu.VMEM((quarter, pivots), jnp.float32)],
        ),
        out_shape=(jax.ShapeDtypeStruct((quarter, half), jnp.float32),) * (2 * across),
        compiler_params=grant(48),
        cost_estimate=pl.CostEstimate(
            flops=6 * total * width * pivots,
            bytes_accessed=4 * (total * width + width * pivots + total * pivots),
            transcendentals=0,
        ),
        name="couple",
    )(where, full, panel_high, panel_low, placed)
    shares_a, shares_b = shares[:across], shares[across:]

    def across_sent(shares):
        return [
            lax.ppermute(shares[k], "x", [(i, (i + k) % across) for i in range(across)])
            for k in range(1, across)
        ]

    def nearer(shares, arrived):
        summed = shares[0] + sum(arrived[1:], arrived[0])
        return exchange(summed.reshape(deep, few, half), "z")

    arrived_a = across_sent(shares_a)
    arrived_b = across_sent(shares_b)
    nearer_a = nearer(shares_a, arrived_a)
    own_b, nearer_a = lax.optimization_barrier((shares_b[0], nearer_a))
    shares_b = (own_b, *shares_b[1:])
    nearer_b = nearer(shares_b, arrived_b)
    copies = pl.pallas_call(
        join_kernel,
        out_shape=jax.ShapeDtypeStruct((deep, few, pivots), jnp.float32),
        in_specs=[VMEM, VMEM],
        out_specs=VMEM,
        compiler_params=grant(8),
        name="join",
    )(nearer_a, nearer_b)
    reduced = exchange(copies, "z").reshape(quarter, pivots)
    kept, other = pl.pallas_call(
        solve_kernel,
        grid=(across,),
        out_shape=(jax.ShapeDtypeStruct((across, tall, part, span), jnp.float32),) * 2,
        in_specs=[
            SMEM,
            pl.BlockSpec((quarter, pivots), lambda i: (0, 0)),
            pl.BlockSpec((1, pivots, span), lambda i: (i, 0, 0)),
            pl.BlockSpec((1, pivots, span), lambda i: (i, 0, 0)),
        ],
        out_specs=(pl.BlockSpec((1, tall, part, span), lambda i: (i, 0, 0, 0)),) * 2,
        scratch_shapes=[
            pltpu.VMEM((quarter, pivots), jnp.bfloat16),
            pltpu.VMEM((quarter, pivots), jnp.bfloat16),
        ],
        compiler_params=grant(60),
        name="solve",
    )(core, reduced, inverse_high, inverse_low)
    kept = kept + lax.ppermute(other, "c", [(0, 1), (1, 0)])
    pieces = exchange(kept.reshape(across * tall, part, span), ("x", "y"))
    return pl.pallas_call(
        child_kernel,
        out_shape=jax.ShapeDtypeStruct((srcs, child_len.shape[0] * BLK), jnp.float32),
        in_specs=[SMEM, SMEM, VMEM],
        out_specs=VMEM,
        scratch_shapes=[pltpu.VMEM((srcs, span + BLK), jnp.float32)],
        compiler_params=grant(8),
        name="children",
    )(first, child_len, pieces.reshape(across, tall, part, span))


def solution(mesh):
    piv = mesh.shape["piv"]
    torus = Mesh(mesh.devices.reshape(8, 4, piv // 2, 2), ("z", "x", "y", "c"))
    return jax.shard_map(
        body,
        mesh=torus,
        in_specs=(
            P(PIV, ROWS),
            P(ROWS),
            P(ROWS, PIV),
            P(PIV, ROWS),
            P(None, PIV + ROWS),
            P(ROWS),
            P(ROWS),
        ),
        out_specs=P(PIV, ROWS),
        check_vma=False,
    )
```

```python
import jax
import jax.numpy as jnp
from jax import lax
from jax.experimental import pallas as pl
from jax.experimental.pallas import tpu as pltpu
from jax.sharding import Mesh
from jax.sharding import PartitionSpec as P

BLK = 128
ROWS = ("z", "x")
PIV = ("y", "c")
VMEM = pl.BlockSpec(memory_space=pltpu.VMEM)
SMEM = pl.BlockSpec(memory_space=pltpu.SMEM)


def grant(size):
    return pltpu.CompilerParams(vmem_limit_bytes=size << 20)


def exchange(value, axes):
    return lax.all_to_all(value, axes, split_axis=0, concat_axis=0, tiled=True)


def spread(value, axis):
    count = lax.axis_size(axis)
    return exchange(jnp.broadcast_to(value[None], (count, *value.shape)), axis)


def pack_kernel(count, maps, where, *rest):
    pieces, sends, column = rest[:-2], rest[-2], rest[-1]
    across, deep = maps.shape[0], column.shape[0]
    for level, piece in enumerate(pieces[:-2]):
        column[level if level < deep // 2 else level + 1] = piece[...]
    upper, lower = pieces[-2:]
    column[deep // 2, : upper.shape[0]] = upper[...]
    column[deep // 2, upper.shape[0] :] = lower[...]
    for dest in range(across):
        for slot in range(count):
            block = maps[dest, slot]
            level = lax.rem(lax.div(block, count * across) - where[0] + deep, deep)
            offset = pl.multiple_of(lax.rem(block, count) * BLK, BLK)
            sends[dest, :, slot * BLK : (slot + 1) * BLK] = column[level, :, pl.ds(offset, BLK)]


def pick_kernel(count, own, arrived, boundary):
    across = arrived.shape[0]
    for slot in range(count):
        origin = lax.rem(lax.div(own[slot], count), across)
        cols = slice(slot * BLK, (slot + 1) * BLK)
        boundary[:, cols] = arrived[origin, :, cols]


def split(value):
    high = value.astype(jnp.bfloat16)
    return high, (value - high.astype(jnp.float32)).astype(jnp.bfloat16)


def product(left, right):
    terms = ((0, 0), (0, 1), (1, 0))
    return sum(jnp.dot(left[i], right[j], preferred_element_type=jnp.float32) for i, j in terms)


def couple_kernel(slots, where, *rest):
    pieces, (panel, placed) = rest[:9], rest[9:11]
    shares, (rows, high, low, total) = rest[11 : 11 + slots], rest[11 + slots :]
    step = pl.program_id(0)

    @pl.when(step == 0)
    def _():
        high[...], low[...] = split(panel[...])

    part = pieces[0].shape[2]
    tall = rows.shape[0] // (2 * part)
    level, core = where[2], where[3]
    way = 1 - 2 * core

    def put(piece, entry, distance, owner):
        at = lax.rem(level + distance + tall, tall)
        rows[pl.ds(pl.multiple_of((at * 2 + owner) * part, part), part)] = piece[entry, 0]

    own, near, far = pieces[0], pieces[1:4], pieces[4:7]
    put(own, 0, 0, core)
    put(own, 1, 0, 1 - core)
    for k in range(3):
        put(near[k], 0, -(k + 1) * way, core)
        put(near[k], 1, -(k + 1) * way, 1 - core)
        put(far[k], 0, (k + 1) * way, 1 - core)
        put(far[k], 1, (k + 1) * way, core)
    put(pieces[7], 0, tall // 2, core)
    put(pieces[8], 0, tall // 2, 1 - core)
    wide = placed.shape[2]
    total[...] = -product(split(rows[...]), (high[...], low[...]))
    window = pl.ds(pl.multiple_of(where[1] * BLK, BLK), wide)
    total[:, window] = total[:, window] + placed[0]
    half = total.shape[1] // 2
    across = slots // 2
    for slot in range(across):

        @pl.when(step == (slot + across - 1) % across)
        def _():
            shares[slot][...] = total[:, :half]
            shares[across + slot][...] = total[:, half:]


def join_kernel(pieces_a, pieces_b, copies):
    first, second = jnp.sum(pieces_a[...], axis=0), jnp.sum(pieces_b[...], axis=0)
    cut = first.shape[1]
    for level in range(copies.shape[0]):
        copies[level, :, :cut] = first
        copies[level, :, cut:] = second


def solve_kernel(core, reduced, inverse_lo, inverse_hi, kept, other, high, low):
    @pl.when(pl.program_id(0) == 0)
    def _():
        high[...], low[...] = split(reduced[...])

    _, tall, part, span = kept.shape
    cut = inverse_lo.shape[1]
    result = product((high[:, :cut], low[:, :cut]), split(inverse_lo[0]))
    result = result + product((high[:, cut:], low[:, cut:]), split(inverse_hi[0]))
    result = result.reshape(tall, 2, part, span)
    first, second = result[:, 0], result[:, 1]
    mine = core[0] == 0
    kept[0] = jnp.where(mine, first, second)
    other[0] = jnp.where(mine, second, first)


def child_kernel(first, length, pieces, children, summed):
    quarters, _, rows, span = pieces.shape
    padded = summed.shape[1]
    for quarter in range(quarters):
        own = slice(quarter * rows, (quarter + 1) * rows)
        summed[own, :span] = jnp.sum(pieces[quarter], axis=0)
    summed[:, span:] = jnp.zeros((quarters * rows, padded - span), jnp.float32)
    lane = lax.broadcasted_iota(jnp.int32, (quarters * rows, BLK), 1)
    for child in range(first.shape[0]):
        offset = jnp.clip(first[child], 0, span - 1)
        tile = lax.div(offset, BLK)
        window = summed[:, pl.ds(pl.multiple_of(tile * BLK, BLK), 2 * BLK)]
        shift = lax.rem(2 * BLK - (offset - tile * BLK), 2 * BLK)
        moved = pltpu.roll(window, shift, 1)[:, :BLK]
        children[:, child * BLK : (child + 1) * BLK] = jnp.where(
            lane < length[child], moved, jnp.zeros_like(moved)
        )


def body(ancestor_sol, front_map, lower_panel, inverse_factor, right_side, child_start, child_len):
    deep, across, tall, cores = (lax.axis_size(a) for a in ("z", "x", "y", "c"))
    srcs, width = ancestor_sol.shape
    count = front_map.shape[0]
    pivots, span = inverse_factor.shape
    total = right_side.shape[0]
    piv_devs = tall * cores
    part = srcs // across
    quarter = total // across
    me = lax.axis_index(ROWS)

    half = pivots // 2
    cut = pivots // 96 * 40
    core = lax.axis_index("c")
    first = child_start - me * span

    def ring(value, axis, hops):
        length = lax.axis_size(axis)
        return lax.ppermute(value, axis, [(i, (i + hops) % length) for i in range(length)])

    maps = spread(front_map, "x").reshape(across, count)
    down_2, up_2 = ring(ancestor_sol, "z", 2), ring(ancestor_sol, "z", -2)
    down_1, up_1 = ring(ancestor_sol, "z", 1), ring(ancestor_sol, "z", -1)
    inverse_lo = spread(inverse_factor[:cut], "x")
    mid = srcs // 2
    upper, lower = ring(down_2[:mid], "z", 2), ring(up_2[mid:], "z", -2)
    down_3, up_3 = ring(down_2, "z", 1), ring(up_2, "z", -1)
    column = (ancestor_sol, up_1, up_2, up_3, down_3, down_2, down_1, upper, lower)
    column, maps, first = lax.optimization_barrier((column, maps, first))
    sends = pl.pallas_call(
        lambda *refs: pack_kernel(count, *refs),
        out_shape=jax.ShapeDtypeStruct((across, srcs, width), jnp.float32),
        in_specs=[SMEM, SMEM] + [VMEM] * len(column),
        out_specs=VMEM,
        scratch_shapes=[pltpu.VMEM((deep, srcs, width), jnp.float32)],
        compiler_params=grant(12),
        name="pack",
    )(maps, lax.axis_index("z").reshape(1), *column)
    sends, inverse_lo = lax.optimization_barrier((sends, inverse_lo))
    arrived = exchange(sends, "x")
    boundary = pl.pallas_call(
        lambda *refs: pick_kernel(count, *refs),
        out_shape=jax.ShapeDtypeStruct((srcs, width), jnp.float32),
        in_specs=[SMEM, VMEM],
        out_specs=VMEM,
        compiler_params=grant(8),
        name="pick",
    )(front_map, arrived)
    boundary, rest, right_side = lax.optimization_barrier(
        (boundary, inverse_factor[cut:], right_side)
    )

    def swap(value):
        return lax.ppermute(value, "c", [(0, 1), (1, 0)])

    def apart(value, hops):
        pairs = [
            (2 * y + c, 2 * ((y + (hops, -hops)[c]) % tall) + c)
            for y in range(tall)
            for c in range(cores)
        ]
        return lax.ppermute(value, PIV, pairs)

    chip = jnp.stack([boundary, swap(boundary)])
    near_2, near_1 = apart(chip, 2), apart(chip, 1)
    inverse_hi = spread(rest, "x")
    near_4, near_3 = apart(near_2[0], 2), apart(near_2, 1)
    far_2, far_1, far_4, far_3 = swap(near_2), swap(near_1), swap(near_4), swap(near_3)
    own_share = right_side.shape[1]
    tile = jnp.minimum(lax.div(me * own_share, BLK), pivots // BLK - 2)
    place = (
        jnp.arange(2 * BLK, dtype=jnp.int32)[None, :]
        == me * own_share - tile * BLK + jnp.arange(own_share, dtype=jnp.int32)[:, None]
    ).astype(jnp.float32)
    ordered = right_side.reshape(piv_devs, across, part, own_share).swapaxes(0, 1)
    placed = jnp.dot(
        ordered.reshape(total, own_share),
        place,
        precision=lax.Precision.HIGHEST,
        preferred_element_type=jnp.float32,
    ).reshape(across, quarter, 2 * BLK)
    pieces = (chip, near_1, near_2, near_3, far_1, far_2, far_3, near_4, far_4)
    pieces, inverse_hi, placed = lax.optimization_barrier((pieces, inverse_hi, placed))
    pieces = [piece.reshape(-1, across, part, width) for piece in pieces]
    few = quarter // deep
    where = jnp.stack([lax.axis_index("x"), tile, lax.axis_index("y"), core])

    def turn(i, at):
        return (lax.rem(at[0] + 1 + i, across), 0, 0)

    shares = pl.pallas_call(
        lambda *refs: couple_kernel(2 * across, *refs),
        grid_spec=pltpu.PrefetchScalarGridSpec(
            num_scalar_prefetch=1,
            grid=(across,),
            in_specs=[
                pl.BlockSpec(
                    (piece.shape[0], 1, part, width), lambda i, at: (0, turn(i, at)[0], 0, 0)
                )
                for piece in pieces
            ]
            + [
                pl.BlockSpec((width, pivots), lambda i, at: (0, 0)),
                pl.BlockSpec((1, quarter, 2 * BLK), turn),
            ],
            out_specs=(pl.BlockSpec((quarter, half), lambda i, at: (0, 0)),) * (2 * across),
            scratch_shapes=[
                pltpu.VMEM((quarter, width), jnp.float32),
                pltpu.VMEM((width, pivots), jnp.bfloat16),
                pltpu.VMEM((width, pivots), jnp.bfloat16),
                pltpu.VMEM((quarter, pivots), jnp.float32),
            ],
        ),
        out_shape=(jax.ShapeDtypeStruct((quarter, half), jnp.float32),) * (2 * across),
        compiler_params=grant(48),
        cost_estimate=pl.CostEstimate(
            flops=6 * total * width * pivots,
            bytes_accessed=4 * (total * width + width * pivots + total * pivots),
            transcendentals=0,
        ),
        name="couple",
    )(where, *pieces, lower_panel, placed)
    shares_a, shares_b = shares[:across], shares[across:]

    def across_sent(shares):
        return [
            lax.ppermute(shares[k], "x", [(i, (i + k) % across) for i in range(across)])
            for k in range(1, across)
        ]

    def nearer(shares, arrived):
        summed = shares[0] + sum(arrived[1:], arrived[0])
        return exchange(summed.reshape(deep, few, half), "z")

    arrived_a = across_sent(shares_a)
    arrived_b = across_sent(shares_b)
    nearer_a = nearer(shares_a, arrived_a)
    own_b, nearer_a = lax.optimization_barrier((shares_b[0], nearer_a))
    shares_b = (own_b, *shares_b[1:])
    nearer_b = nearer(shares_b, arrived_b)
    copies = pl.pallas_call(
        join_kernel,
        out_shape=jax.ShapeDtypeStruct((deep, few, pivots), jnp.float32),
        in_specs=[VMEM, VMEM],
        out_specs=VMEM,
        compiler_params=grant(8),
        name="join",
    )(nearer_a, nearer_b)
    reduced = exchange(copies, "z").reshape(quarter, pivots)
    kept, other = pl.pallas_call(
        solve_kernel,
        grid=(across,),
        out_shape=(jax.ShapeDtypeStruct((across, tall, part, span), jnp.float32),) * 2,
        in_specs=[
            SMEM,
            pl.BlockSpec((quarter, pivots), lambda i: (0, 0)),
            pl.BlockSpec((1, cut, span), lambda i: (i, 0, 0)),
            pl.BlockSpec((1, pivots - cut, span), lambda i: (i, 0, 0)),
        ],
        out_specs=(pl.BlockSpec((1, tall, part, span), lambda i: (i, 0, 0, 0)),) * 2,
        scratch_shapes=[
            pltpu.VMEM((quarter, pivots), jnp.bfloat16),
            pltpu.VMEM((quarter, pivots), jnp.bfloat16),
        ],
        compiler_params=grant(60),
        name="solve",
    )(
        core.reshape(1),
        reduced,
        inverse_lo.reshape(across, cut, span),
        inverse_hi.reshape(across, pivots - cut, span),
    )
    kept = kept + swap(other)
    arrived = exchange(kept.reshape(across * tall, part, span), ("x", "y"))
    return pl.pallas_call(
        child_kernel,
        out_shape=jax.ShapeDtypeStruct((srcs, child_len.shape[0] * BLK), jnp.float32),
        in_specs=[SMEM, SMEM, VMEM],
        out_specs=VMEM,
        scratch_shapes=[pltpu.VMEM((srcs, span + BLK), jnp.float32)],
        compiler_params=grant(8),
        name="children",
    )(first, child_len, arrived.reshape(across, tall, part, span))


def solution(mesh):
    piv = mesh.shape["piv"]
    torus = Mesh(mesh.devices.reshape(8, 4, piv // 2, 2), ("z", "x", "y", "c"))
    return jax.shard_map(
        body,
        mesh=torus,
        in_specs=(
            P(PIV, ROWS),
            P(ROWS),
            P(ROWS, PIV),
            P(PIV, ROWS),
            P(None, PIV + ROWS),
            P(ROWS),
            P(ROWS),
        ),
        out_specs=P(PIV, ROWS),
        check_vma=False,
    )
```

```python
import jax
import jax.numpy as jnp
from jax import lax
from jax.experimental import pallas as pl
from jax.experimental.pallas import tpu as pltpu
from jax.sharding import Mesh
from jax.sharding import PartitionSpec as P

BLK = 128
ROWS = ("z", "x")
PIV = ("y", "c")
VMEM = pl.BlockSpec(memory_space=pltpu.VMEM)
SMEM = pl.BlockSpec(memory_space=pltpu.SMEM)


def grant(size):
    return pltpu.CompilerParams(vmem_limit_bytes=size << 20)


def exchange(value, axes):
    return lax.all_to_all(value, axes, split_axis=0, concat_axis=0, tiled=True)


def spread(value, axis):
    count = lax.axis_size(axis)
    return exchange(jnp.broadcast_to(value[None], (count, *value.shape)), axis)


def pack_kernel(count, maps, where, *rest):
    pieces, sends, column = rest[:-2], rest[-2], rest[-1]
    across, deep = maps.shape[0], column.shape[0]
    for level, piece in enumerate(pieces[:-2]):
        column[level if level < deep // 2 else level + 1] = piece[...]
    upper, lower = pieces[-2:]
    column[deep // 2, : upper.shape[0]] = upper[...]
    column[deep // 2, upper.shape[0] :] = lower[...]
    for dest in range(across):
        for slot in range(count):
            block = maps[dest, slot]
            level = lax.rem(lax.div(block, count * across) - where[0] + deep, deep)
            offset = pl.multiple_of(lax.rem(block, count) * BLK, BLK)
            sends[dest, :, slot * BLK : (slot + 1) * BLK] = column[level, :, pl.ds(offset, BLK)]


def pick_kernel(count, own, arrived, boundary):
    across = arrived.shape[0]
    for slot in range(count):
        origin = lax.rem(lax.div(own[slot], count), across)
        cols = slice(slot * BLK, (slot + 1) * BLK)
        boundary[:, cols] = arrived[origin, :, cols]


def split(value):
    high = value.astype(jnp.bfloat16)
    return high, (value - high.astype(jnp.float32)).astype(jnp.bfloat16)


def product(left, right):
    terms = ((0, 0), (0, 1), (1, 0))
    return sum(jnp.dot(left[i], right[j], preferred_element_type=jnp.float32) for i, j in terms)


def halve_kernel(value, high, low):
    high[...], low[...] = split(value[...])


def couple_kernel(slots, where, *rest):
    pieces, (high, low, placed) = rest[:9], rest[9:12]
    shares, (rows, total) = rest[12 : 12 + slots], rest[12 + slots :]
    step = pl.program_id(0)
    part = pieces[0].shape[2]
    tall = rows.shape[0] // (2 * part)
    level, core = where[2], where[3]
    way = 1 - 2 * core

    def put(piece, entry, distance, owner):
        at = lax.rem(level + distance + tall, tall)
        rows[pl.ds(pl.multiple_of((at * 2 + owner) * part, part), part)] = piece[entry, 0]

    own, near, far = pieces[0], pieces[1:4], pieces[4:7]
    put(own, 0, 0, core)
    put(own, 1, 0, 1 - core)
    for k in range(3):
        put(near[k], 0, -(k + 1) * way, core)
        put(near[k], 1, -(k + 1) * way, 1 - core)
        put(far[k], 0, (k + 1) * way, 1 - core)
        put(far[k], 1, (k + 1) * way, core)
    put(pieces[7], 0, tall // 2, core)
    put(pieces[8], 0, tall // 2, 1 - core)
    wide = placed.shape[2]
    total[...] = -product(split(rows[...]), (high[...], low[...]))
    window = pl.ds(pl.multiple_of(where[1] * BLK, BLK), wide)
    total[:, window] = total[:, window] + placed[0]
    half = total.shape[1] // 2
    across = slots // 2
    for slot in range(across):

        @pl.when(step == (slot + across - 1) % across)
        def _():
            shares[slot][...] = total[:, :half]
            shares[across + slot][...] = total[:, half:]


def join_kernel(pieces_a, pieces_b, copies):
    first, second = jnp.sum(pieces_a[...], axis=0), jnp.sum(pieces_b[...], axis=0)
    cut = first.shape[1]
    for level in range(copies.shape[0]):
        copies[level, :, :cut] = first
        copies[level, :, cut:] = second


def solve_kernel(core, reduced, inverse_lo, inverse_hi, kept, other, high, low):
    @pl.when(pl.program_id(0) == 0)
    def _():
        high[...], low[...] = split(reduced[...])

    _, tall, part, span = kept.shape
    cut = inverse_lo.shape[1]
    result = product((high[:, :cut], low[:, :cut]), split(inverse_lo[0]))
    result = result + product((high[:, cut:], low[:, cut:]), split(inverse_hi[0]))
    result = result.reshape(tall, 2, part, span)
    first, second = result[:, 0], result[:, 1]
    mine = core[0] == 0
    kept[0] = jnp.where(mine, first, second)
    other[0] = jnp.where(mine, second, first)


def child_kernel(first, length, pieces, children, summed):
    quarters, _, rows, span = pieces.shape
    padded = summed.shape[1]
    for quarter in range(quarters):
        own = slice(quarter * rows, (quarter + 1) * rows)
        summed[own, :span] = jnp.sum(pieces[quarter], axis=0)
    summed[:, span:] = jnp.zeros((quarters * rows, padded - span), jnp.float32)
    lane = lax.broadcasted_iota(jnp.int32, (quarters * rows, BLK), 1)
    for child in range(first.shape[0]):
        offset = jnp.clip(first[child], 0, span - 1)
        tile = lax.div(offset, BLK)
        window = summed[:, pl.ds(pl.multiple_of(tile * BLK, BLK), 2 * BLK)]
        shift = lax.rem(2 * BLK - (offset - tile * BLK), 2 * BLK)
        moved = pltpu.roll(window, shift, 1)[:, :BLK]
        children[:, child * BLK : (child + 1) * BLK] = jnp.where(
            lane < length[child], moved, jnp.zeros_like(moved)
        )


def body(ancestor_sol, front_map, lower_panel, inverse_factor, right_side, child_start, child_len):
    deep, across, tall, cores = (lax.axis_size(a) for a in ("z", "x", "y", "c"))
    srcs, width = ancestor_sol.shape
    count = front_map.shape[0]
    pivots, span = inverse_factor.shape
    total = right_side.shape[0]
    piv_devs = tall * cores
    part = srcs // across
    quarter = total // across
    me = lax.axis_index(ROWS)

    half = pivots // 2
    cut = pivots // 96 * 44
    core = lax.axis_index("c")
    first = child_start - me * span

    def ring(value, axis, hops):
        length = lax.axis_size(axis)
        return lax.ppermute(value, axis, [(i, (i + hops) % length) for i in range(length)])

    down_2, up_2 = ring(ancestor_sol, "z", 2), ring(ancestor_sol, "z", -2)
    down_1, up_1 = ring(ancestor_sol, "z", 1), ring(ancestor_sol, "z", -1)
    rows = jnp.broadcast_to(front_map.astype(jnp.float32)[:, None], (count, span))
    inverse_lo = spread(jnp.concatenate([inverse_factor[:cut], rows]), "x")
    inverse_lo = inverse_lo.reshape(across, cut + count, span)
    maps = inverse_lo[:, cut:, 0].astype(jnp.int32)
    mid = srcs // 2
    upper, lower = ring(down_2[:mid], "z", 2), ring(up_2[mid:], "z", -2)
    down_3, up_3 = ring(down_2, "z", 1), ring(up_2, "z", -1)
    column = (ancestor_sol, up_1, up_2, up_3, down_3, down_2, down_1, upper, lower)
    column, maps, first = lax.optimization_barrier((column, maps, first))
    sends = pl.pallas_call(
        lambda *refs: pack_kernel(count, *refs),
        out_shape=jax.ShapeDtypeStruct((across, srcs, width), jnp.float32),
        in_specs=[SMEM, SMEM] + [VMEM] * len(column),
        out_specs=VMEM,
        scratch_shapes=[pltpu.VMEM((deep, srcs, width), jnp.float32)],
        compiler_params=grant(12),
        name="pack",
    )(maps, lax.axis_index("z").reshape(1), *column)
    sends, inverse_lo, rest, right_side, lower_panel = lax.optimization_barrier(
        (sends, inverse_lo, inverse_factor[cut:], right_side, lower_panel)
    )
    arrived = exchange(sends, "x")
    rest = jnp.broadcast_to(rest[None], (across, *rest.shape))
    panel_high, panel_low = pl.pallas_call(
        halve_kernel,
        grid=(4,),
        out_shape=(jax.ShapeDtypeStruct((width, pivots), jnp.bfloat16),) * 2,
        in_specs=[pl.BlockSpec((width // 4, pivots), lambda i: (i, 0))],
        out_specs=(pl.BlockSpec((width // 4, pivots), lambda i: (i, 0)),) * 2,
        compiler_params=grant(60),
        cost_estimate=pl.CostEstimate(
            flops=4 * width * pivots, bytes_accessed=8 * width * pivots, transcendentals=0
        ),
        name="halve",
    )(lower_panel)
    own_share = right_side.shape[1]
    tile = jnp.minimum(lax.div(me * own_share, BLK), pivots // BLK - 2)
    place = (
        jnp.arange(2 * BLK, dtype=jnp.int32)[None, :]
        == me * own_share - tile * BLK + jnp.arange(own_share, dtype=jnp.int32)[:, None]
    ).astype(jnp.float32)
    ordered = right_side.reshape(piv_devs, across, part, own_share).swapaxes(0, 1)
    placed = jnp.dot(
        ordered.reshape(total, own_share),
        place,
        precision=lax.Precision.HIGHEST,
        preferred_element_type=jnp.float32,
    ).reshape(across, quarter, 2 * BLK)
    boundary = pl.pallas_call(
        lambda *refs: pick_kernel(count, *refs),
        out_shape=jax.ShapeDtypeStruct((srcs, width), jnp.float32),
        in_specs=[SMEM, VMEM],
        out_specs=VMEM,
        compiler_params=grant(8),
        name="pick",
    )(front_map, arrived)
    boundary, rest, placed, panel_high, panel_low = lax.optimization_barrier(
        (boundary, rest, placed, panel_high, panel_low)
    )

    def swap(value):
        return lax.ppermute(value, "c", [(0, 1), (1, 0)])

    def apart(value, hops):
        pairs = [
            (2 * y + c, 2 * ((y + (hops, -hops)[c]) % tall) + c)
            for y in range(tall)
            for c in range(cores)
        ]
        return lax.ppermute(value, PIV, pairs)

    chip = jnp.stack([boundary, swap(boundary)])
    near_2, near_1 = apart(chip, 2), apart(chip, 1)
    inverse_hi = exchange(rest, "x")
    near_4, near_3 = apart(near_2[0], 2), apart(near_2, 1)
    far_2, far_1, far_4, far_3 = swap(near_2), swap(near_1), swap(near_4), swap(near_3)
    pieces = (chip, near_1, near_2, near_3, far_1, far_2, far_3, near_4, far_4)
    pieces = [piece.reshape(-1, across, part, width) for piece in pieces]
    few = quarter // deep
    where = jnp.stack([lax.axis_index("x"), tile, lax.axis_index("y"), core])

    def turn(i, at):
        return (lax.rem(at[0] + 1 + i, across), 0, 0)

    shares = pl.pallas_call(
        lambda *refs: couple_kernel(2 * across, *refs),
        grid_spec=pltpu.PrefetchScalarGridSpec(
            num_scalar_prefetch=1,
            grid=(across,),
            in_specs=[
                pl.BlockSpec(
                    (piece.shape[0], 1, part, width), lambda i, at: (0, turn(i, at)[0], 0, 0)
                )
                for piece in pieces
            ]
            + [
                pl.BlockSpec((width, pivots), lambda i, at: (0, 0)),
                pl.BlockSpec((width, pivots), lambda i, at: (0, 0)),
                pl.BlockSpec((1, quarter, 2 * BLK), turn),
            ],
            out_specs=(pl.BlockSpec((quarter, half), lambda i, at: (0, 0)),) * (2 * across),
            scratch_shapes=[
                pltpu.VMEM((quarter, width), jnp.float32),
                pltpu.VMEM((quarter, pivots), jnp.float32),
            ],
        ),
        out_shape=(jax.ShapeDtypeStruct((quarter, half), jnp.float32),) * (2 * across),
        compiler_params=grant(48),
        cost_estimate=pl.CostEstimate(
            flops=6 * total * width * pivots,
            bytes_accessed=4 * (total * width + width * pivots + total * pivots),
            transcendentals=0,
        ),
        name="couple",
    )(where, *pieces, panel_high, panel_low, placed)
    shares_a, shares_b = shares[:across], shares[across:]

    def across_sent(shares):
        return [
            lax.ppermute(shares[k], "x", [(i, (i + k) % across) for i in range(across)])
            for k in range(1, across)
        ]

    def nearer(shares, arrived):
        summed = shares[0] + sum(arrived[1:], arrived[0])
        return exchange(summed.reshape(deep, few, half), "z")

    arrived_a = across_sent(shares_a)
    arrived_b = across_sent(shares_b)
    own_a, inverse_hi = lax.optimization_barrier((shares_a[0], inverse_hi))
    shares_a = (own_a, *shares_a[1:])
    nearer_a = nearer(shares_a, arrived_a)
    own_b, nearer_a = lax.optimization_barrier((shares_b[0], nearer_a))
    shares_b = (own_b, *shares_b[1:])
    nearer_b = nearer(shares_b, arrived_b)
    copies = pl.pallas_call(
        join_kernel,
        out_shape=jax.ShapeDtypeStruct((deep, few, pivots), jnp.float32),
        in_specs=[VMEM, VMEM],
        out_specs=VMEM,
        compiler_params=grant(8),
        name="join",
    )(nearer_a, nearer_b)
    reduced = exchange(copies, "z").reshape(quarter, pivots)
    kept, other = pl.pallas_call(
        solve_kernel,
        grid=(across,),
        out_shape=(jax.ShapeDtypeStruct((across, tall, part, span), jnp.float32),) * 2,
        in_specs=[
            SMEM,
            pl.BlockSpec((quarter, pivots), lambda i: (0, 0)),
            pl.BlockSpec((1, cut, span), lambda i: (i, 0, 0)),
            pl.BlockSpec((1, pivots - cut, span), lambda i: (i, 0, 0)),
        ],
        out_specs=(pl.BlockSpec((1, tall, part, span), lambda i: (i, 0, 0, 0)),) * 2,
        scratch_shapes=[
            pltpu.VMEM((quarter, pivots), jnp.bfloat16),
            pltpu.VMEM((quarter, pivots), jnp.bfloat16),
        ],
        compiler_params=grant(60),
        name="solve",
    )(
        core.reshape(1),
        reduced,
        inverse_lo,
        inverse_hi,
    )
    kept = kept + swap(other)
    arrived = exchange(kept.reshape(across * tall, part, span), ("x", "y"))
    return pl.pallas_call(
        child_kernel,
        out_shape=jax.ShapeDtypeStruct((srcs, child_len.shape[0] * BLK), jnp.float32),
        in_specs=[SMEM, SMEM, VMEM],
        out_specs=VMEM,
        scratch_shapes=[pltpu.VMEM((srcs, span + BLK), jnp.float32)],
        compiler_params=grant(8),
        name="children",
    )(first, child_len, arrived.reshape(across, tall, part, span))


def solution(mesh):
    piv = mesh.shape["piv"]
    torus = Mesh(mesh.devices.reshape(8, 4, piv // 2, 2), ("z", "x", "y", "c"))
    return jax.shard_map(
        body,
        mesh=torus,
        in_specs=(
            P(PIV, ROWS),
            P(ROWS),
            P(ROWS, PIV),
            P(PIV, ROWS),
            P(None, PIV + ROWS),
            P(ROWS),
            P(ROWS),
        ),
        out_specs=P(PIV, ROWS),
        check_vma=False,
    )
```

```python
import jax
import jax.numpy as jnp
from jax import lax
from jax.experimental import pallas as pl
from jax.experimental.pallas import tpu as pltpu
from jax.sharding import Mesh
from jax.sharding import PartitionSpec as P

BLK = 128
ROWS = ("z", "x")
PIV = ("y", "c")
VMEM = pl.BlockSpec(memory_space=pltpu.VMEM)
SMEM = pl.BlockSpec(memory_space=pltpu.SMEM)


def grant(size):
    return pltpu.CompilerParams(vmem_limit_bytes=size << 20)


def exchange(value, axes):
    return lax.all_to_all(value, axes, split_axis=0, concat_axis=0, tiled=True)


def pack_kernel(count, maps, where, *rest):
    pieces, sends, column = rest[:-2], rest[-2], rest[-1]
    across, deep = maps.shape[0], column.shape[0]
    for level, piece in enumerate(pieces[:-2]):
        column[level if level < deep // 2 else level + 1] = piece[...]
    upper, lower = pieces[-2:]
    column[deep // 2, : upper.shape[0]] = upper[...]
    column[deep // 2, upper.shape[0] :] = lower[...]
    for dest in range(across):
        for slot in range(count):
            block = maps[dest, slot]
            level = lax.rem(lax.div(block, count * across) - where[0] + deep, deep)
            offset = pl.multiple_of(lax.rem(block, count) * BLK, BLK)
            sends[dest, :, slot * BLK : (slot + 1) * BLK] = column[level, :, pl.ds(offset, BLK)]


def pick_kernel(count, own, arrived, boundary):
    across = arrived.shape[0]
    for slot in range(count):
        origin = lax.rem(lax.div(own[slot], count), across)
        cols = slice(slot * BLK, (slot + 1) * BLK)
        boundary[:, cols] = arrived[origin, :, cols]


def split(value):
    high = value.astype(jnp.bfloat16)
    return high, (value - high.astype(jnp.float32)).astype(jnp.bfloat16)


def product(left, right):
    terms = ((0, 0), (0, 1), (1, 0))
    return sum(jnp.dot(left[i], right[j], preferred_element_type=jnp.float32) for i, j in terms)


def repeat_kernel(own, inverse, repeated):
    _, rows, span = repeated.shape
    cut = inverse.shape[0]
    repeated[0, :cut] = inverse[...]
    for block in range(rows - cut):
        value = own[block].astype(jnp.float32)
        repeated[0, cut + block : cut + block + 1] = jnp.full((1, span), value, jnp.float32)


def copy_kernel(inverse, repeated):
    repeated[0] = inverse[...]


def halve_kernel(value, high, low):
    high[...], low[...] = split(value[...])


def couple_kernel(slots, where, *rest):
    pieces, (high, low, placed) = rest[:9], rest[9:12]
    shares, (rows, total) = rest[12 : 12 + slots], rest[12 + slots :]
    step = pl.program_id(0)
    part = pieces[0].shape[2]
    tall = rows.shape[0] // (2 * part)
    level, core = where[2], where[3]
    way = 1 - 2 * core

    def put(piece, entry, distance, owner):
        at = lax.rem(level + distance + tall, tall)
        rows[pl.ds(pl.multiple_of((at * 2 + owner) * part, part), part)] = piece[entry, 0]

    own, near, far = pieces[0], pieces[1:4], pieces[4:7]
    put(own, 0, 0, core)
    put(own, 1, 0, 1 - core)
    for k in range(3):
        put(near[k], 0, -(k + 1) * way, core)
        put(near[k], 1, -(k + 1) * way, 1 - core)
        put(far[k], 0, (k + 1) * way, 1 - core)
        put(far[k], 1, (k + 1) * way, core)
    put(pieces[7], 0, tall // 2, core)
    put(pieces[8], 0, tall // 2, 1 - core)
    wide = placed.shape[2]
    total[...] = -product(split(rows[...]), (high[...], low[...]))
    window = pl.ds(pl.multiple_of(where[1] * BLK, BLK), wide)
    total[:, window] = total[:, window] + placed[0]
    half = total.shape[1] // 2
    across = slots // 2
    for slot in range(across):

        @pl.when(step == (slot + across - 1) % across)
        def _():
            shares[slot][...] = total[:, :half]
            shares[across + slot][...] = total[:, half:]


def join_kernel(pieces_a, pieces_b, copies):
    first, second = jnp.sum(pieces_a[...], axis=0), jnp.sum(pieces_b[...], axis=0)
    cut = first.shape[1]
    for level in range(copies.shape[0]):
        copies[level, :, :cut] = first
        copies[level, :, cut:] = second


def solve_kernel(core, reduced, inverse_lo, inverse_hi, kept, other, high, low):
    @pl.when(pl.program_id(0) == 0)
    def _():
        high[...], low[...] = split(reduced[...])

    _, tall, part, span = kept.shape
    cut = inverse_lo.shape[1]
    result = product((high[:, :cut], low[:, :cut]), split(inverse_lo[0]))
    result = result + product((high[:, cut:], low[:, cut:]), split(inverse_hi[0]))
    result = result.reshape(tall, 2, part, span)
    first, second = result[:, 0], result[:, 1]
    mine = core[0] == 0
    kept[0] = jnp.where(mine, first, second)
    other[0] = jnp.where(mine, second, first)


def child_kernel(first, length, pieces, children, summed):
    quarters, _, rows, span = pieces.shape
    padded = summed.shape[1]
    for quarter in range(quarters):
        own = slice(quarter * rows, (quarter + 1) * rows)
        summed[own, :span] = jnp.sum(pieces[quarter], axis=0)
    summed[:, span:] = jnp.zeros((quarters * rows, padded - span), jnp.float32)
    lane = lax.broadcasted_iota(jnp.int32, (quarters * rows, BLK), 1)
    for child in range(first.shape[0]):
        offset = jnp.clip(first[child], 0, span - 1)
        tile = lax.div(offset, BLK)
        window = summed[:, pl.ds(pl.multiple_of(tile * BLK, BLK), 2 * BLK)]
        shift = lax.rem(2 * BLK - (offset - tile * BLK), 2 * BLK)
        moved = pltpu.roll(window, shift, 1)[:, :BLK]
        children[:, child * BLK : (child + 1) * BLK] = jnp.where(
            lane < length[child], moved, jnp.zeros_like(moved)
        )


def body(ancestor_sol, front_map, lower_panel, inverse_factor, right_side, child_start, child_len):
    deep, across, tall, cores = (lax.axis_size(a) for a in ("z", "x", "y", "c"))
    srcs, width = ancestor_sol.shape
    count = front_map.shape[0]
    pivots, span = inverse_factor.shape
    total = right_side.shape[0]
    piv_devs = tall * cores
    part = srcs // across
    quarter = total // across
    me = lax.axis_index(ROWS)

    half = pivots // 2
    cut = pivots // 3
    core = lax.axis_index("c")
    first = child_start - me * span

    def ring(value, axis, hops):
        length = lax.axis_size(axis)
        return lax.ppermute(value, axis, [(i, (i + hops) % length) for i in range(length)])

    down_2, up_2 = ring(ancestor_sol, "z", 2), ring(ancestor_sol, "z", -2)
    down_1, up_1 = ring(ancestor_sol, "z", 1), ring(ancestor_sol, "z", -1)
    inverse_lo = pl.pallas_call(
        repeat_kernel,
        grid=(across,),
        out_shape=jax.ShapeDtypeStruct((across, cut + count, span), jnp.float32),
        in_specs=[SMEM, pl.BlockSpec((cut, span), lambda i: (0, 0))],
        out_specs=pl.BlockSpec((1, cut + count, span), lambda i: (i, 0, 0)),
        compiler_params=grant(60),
        name="repeat",
    )(front_map, inverse_factor)
    inverse_lo = exchange(inverse_lo, "x")
    maps = inverse_lo[:, cut:, 0].astype(jnp.int32)
    mid = srcs // 2
    upper, lower = ring(down_2[:mid], "z", 2), ring(up_2[mid:], "z", -2)
    down_3, up_3 = ring(down_2, "z", 1), ring(up_2, "z", -1)
    column = (ancestor_sol, up_1, up_2, up_3, down_3, down_2, down_1, upper, lower)
    column, maps, first = lax.optimization_barrier((column, maps, first))
    sends = pl.pallas_call(
        lambda *refs: pack_kernel(count, *refs),
        out_shape=jax.ShapeDtypeStruct((across, srcs, width), jnp.float32),
        in_specs=[SMEM, SMEM] + [VMEM] * len(column),
        out_specs=VMEM,
        scratch_shapes=[pltpu.VMEM((deep, srcs, width), jnp.float32)],
        compiler_params=grant(12),
        name="pack",
    )(maps, lax.axis_index("z").reshape(1), *column)
    sends, inverse_lo, inverse_factor, right_side, lower_panel = lax.optimization_barrier(
        (sends, inverse_lo, inverse_factor, right_side, lower_panel)
    )
    arrived = exchange(sends, "x")
    rest = pl.pallas_call(
        copy_kernel,
        grid=(pivots // cut - 1, across),
        out_shape=jax.ShapeDtypeStruct((across, pivots - cut, span), jnp.float32),
        in_specs=[pl.BlockSpec((cut, span), lambda j, i: (j + 1, 0))],
        out_specs=pl.BlockSpec((1, cut, span), lambda j, i: (i, j, 0)),
        compiler_params=grant(60),
        cost_estimate=pl.CostEstimate(
            flops=pivots * span, bytes_accessed=5 * 4 * pivots * span, transcendentals=0
        ),
        name="copies",
    )(inverse_factor)
    panel_high, panel_low = pl.pallas_call(
        halve_kernel,
        grid=(4,),
        out_shape=(jax.ShapeDtypeStruct((width, pivots), jnp.bfloat16),) * 2,
        in_specs=[pl.BlockSpec((width // 4, pivots), lambda i: (i, 0))],
        out_specs=(pl.BlockSpec((width // 4, pivots), lambda i: (i, 0)),) * 2,
        compiler_params=grant(60),
        cost_estimate=pl.CostEstimate(
            flops=4 * width * pivots, bytes_accessed=8 * width * pivots, transcendentals=0
        ),
        name="halve",
    )(lower_panel)
    own_share = right_side.shape[1]
    tile = jnp.minimum(lax.div(me * own_share, BLK), pivots // BLK - 2)
    place = (
        jnp.arange(2 * BLK, dtype=jnp.int32)[None, :]
        == me * own_share - tile * BLK + jnp.arange(own_share, dtype=jnp.int32)[:, None]
    ).astype(jnp.float32)
    ordered = right_side.reshape(piv_devs, across, part, own_share).swapaxes(0, 1)
    placed = jnp.dot(
        ordered.reshape(total, own_share),
        place,
        precision=lax.Precision.HIGHEST,
        preferred_element_type=jnp.float32,
    ).reshape(across, quarter, 2 * BLK)
    boundary = pl.pallas_call(
        lambda *refs: pick_kernel(count, *refs),
        out_shape=jax.ShapeDtypeStruct((srcs, width), jnp.float32),
        in_specs=[SMEM, VMEM],
        out_specs=VMEM,
        compiler_params=grant(8),
        name="pick",
    )(front_map, arrived)
    boundary, rest, placed, panel_high, panel_low = lax.optimization_barrier(
        (boundary, rest, placed, panel_high, panel_low)
    )

    def swap(value):
        return lax.ppermute(value, "c", [(0, 1), (1, 0)])

    def apart(value, hops):
        pairs = [
            (2 * y + c, 2 * ((y + (hops, -hops)[c]) % tall) + c)
            for y in range(tall)
            for c in range(cores)
        ]
        return lax.ppermute(value, PIV, pairs)

    chip = jnp.stack([boundary, swap(boundary)])
    near_2, near_1 = apart(chip, 2), apart(chip, 1)
    inverse_hi = exchange(rest, "x")
    near_4, near_3 = apart(near_2[0], 2), apart(near_2, 1)
    far_2, far_1, far_4, far_3 = swap(near_2), swap(near_1), swap(near_4), swap(near_3)
    pieces = (chip, near_1, near_2, near_3, far_1, far_2, far_3, near_4, far_4)
    pieces = [piece.reshape(-1, across, part, width) for piece in pieces]
    few = quarter // deep
    where = jnp.stack([lax.axis_index("x"), tile, lax.axis_index("y"), core])

    def turn(i, at):
        return (lax.rem(at[0] + 1 + i, across), 0, 0)

    shares = pl.pallas_call(
        lambda *refs: couple_kernel(2 * across, *refs),
        grid_spec=pltpu.PrefetchScalarGridSpec(
            num_scalar_prefetch=1,
            grid=(across,),
            in_specs=[
                pl.BlockSpec(
                    (piece.shape[0], 1, part, width), lambda i, at: (0, turn(i, at)[0], 0, 0)
                )
                for piece in pieces
            ]
            + [
                pl.BlockSpec((width, pivots), lambda i, at: (0, 0)),
                pl.BlockSpec((width, pivots), lambda i, at: (0, 0)),
                pl.BlockSpec((1, quarter, 2 * BLK), turn),
            ],
            out_specs=(pl.BlockSpec((quarter, half), lambda i, at: (0, 0)),) * (2 * across),
            scratch_shapes=[
                pltpu.VMEM((quarter, width), jnp.float32),
                pltpu.VMEM((quarter, pivots), jnp.float32),
            ],
        ),
        out_shape=(jax.ShapeDtypeStruct((quarter, half), jnp.float32),) * (2 * across),
        compiler_params=grant(48),
        cost_estimate=pl.CostEstimate(
            flops=6 * total * width * pivots,
            bytes_accessed=4 * (total * width + width * pivots + total * pivots),
            transcendentals=0,
        ),
        name="couple",
    )(where, *pieces, panel_high, panel_low, placed)
    shares_a, shares_b = shares[:across], shares[across:]

    def across_sent(shares):
        return [
            lax.ppermute(shares[k], "x", [(i, (i + k) % across) for i in range(across)])
            for k in range(1, across)
        ]

    def nearer(shares, arrived):
        summed = shares[0] + sum(arrived[1:], arrived[0])
        return exchange(summed.reshape(deep, few, half), "z")

    arrived_a = across_sent(shares_a)
    arrived_b = across_sent(shares_b)
    own_a, inverse_hi = lax.optimization_barrier((shares_a[0], inverse_hi))
    shares_a = (own_a, *shares_a[1:])
    nearer_a = nearer(shares_a, arrived_a)
    own_b, nearer_a = lax.optimization_barrier((shares_b[0], nearer_a))
    shares_b = (own_b, *shares_b[1:])
    nearer_b = nearer(shares_b, arrived_b)
    copies = pl.pallas_call(
        join_kernel,
        out_shape=jax.ShapeDtypeStruct((deep, few, pivots), jnp.float32),
        in_specs=[VMEM, VMEM],
        out_specs=VMEM,
        compiler_params=grant(8),
        name="join",
    )(nearer_a, nearer_b)
    reduced = exchange(copies, "z").reshape(quarter, pivots)
    kept, other = pl.pallas_call(
        solve_kernel,
        grid=(across,),
        out_shape=(jax.ShapeDtypeStruct((across, tall, part, span), jnp.float32),) * 2,
        in_specs=[
            SMEM,
            pl.BlockSpec((quarter, pivots), lambda i: (0, 0)),
            pl.BlockSpec((1, cut, span), lambda i: (i, 0, 0)),
            pl.BlockSpec((1, pivots - cut, span), lambda i: (i, 0, 0)),
        ],
        out_specs=(pl.BlockSpec((1, tall, part, span), lambda i: (i, 0, 0, 0)),) * 2,
        scratch_shapes=[
            pltpu.VMEM((quarter, pivots), jnp.bfloat16),
            pltpu.VMEM((quarter, pivots), jnp.bfloat16),
        ],
        compiler_params=grant(60),
        name="solve",
    )(
        core.reshape(1),
        reduced,
        inverse_lo,
        inverse_hi,
    )
    kept = kept + swap(other)
    arrived = exchange(kept.reshape(across * tall, part, span), ("x", "y"))
    return pl.pallas_call(
        child_kernel,
        out_shape=jax.ShapeDtypeStruct((srcs, child_len.shape[0] * BLK), jnp.float32),
        in_specs=[SMEM, SMEM, VMEM],
        out_specs=VMEM,
        scratch_shapes=[pltpu.VMEM((srcs, span + BLK), jnp.float32)],
        compiler_params=grant(8),
        name="children",
    )(first, child_len, arrived.reshape(across, tall, part, span))


def solution(mesh):
    piv = mesh.shape["piv"]
    torus = Mesh(mesh.devices.reshape(8, 4, piv // 2, 2), ("z", "x", "y", "c"))
    return jax.shard_map(
        body,
        mesh=torus,
        in_specs=(
            P(PIV, ROWS),
            P(ROWS),
            P(ROWS, PIV),
            P(PIV, ROWS),
            P(None, PIV + ROWS),
            P(ROWS),
            P(ROWS),
        ),
        out_specs=P(PIV, ROWS),
        check_vma=False,
    )
```

```python
import jax
import jax.numpy as jnp
from jax import lax
from jax.experimental import pallas as pl
from jax.experimental.pallas import tpu as pltpu
from jax.sharding import Mesh
from jax.sharding import PartitionSpec as P

BLK = 128
ROWS = ("z", "x")
PIV = ("y", "c")
VMEM = pl.BlockSpec(memory_space=pltpu.VMEM)
SMEM = pl.BlockSpec(memory_space=pltpu.SMEM)


def grant(size):
    return pltpu.CompilerParams(vmem_limit_bytes=size << 20)


def exchange(value, axes):
    return lax.all_to_all(value, axes, split_axis=0, concat_axis=0, tiled=True)


def pack_kernel(count, maps, where, *rest):
    pieces, sends, column = rest[:-2], rest[-2], rest[-1]
    across, deep = maps.shape[0], column.shape[0]
    for level, piece in enumerate(pieces[:-2]):
        column[level if level < deep // 2 else level + 1] = piece[...]
    upper, lower = pieces[-2:]
    column[deep // 2, : upper.shape[0]] = upper[...]
    column[deep // 2, upper.shape[0] :] = lower[...]
    for dest in range(across):
        for slot in range(count):
            block = maps[dest, slot]
            level = lax.rem(lax.div(block, count * across) - where[0] + deep, deep)
            offset = pl.multiple_of(lax.rem(block, count) * BLK, BLK)
            sends[dest, :, slot * BLK : (slot + 1) * BLK] = column[level, :, pl.ds(offset, BLK)]


def pick_kernel(count, own, arrived, boundary):
    across = arrived.shape[0]
    for slot in range(count):
        origin = lax.rem(lax.div(own[slot], count), across)
        cols = slice(slot * BLK, (slot + 1) * BLK)
        boundary[:, cols] = arrived[origin, :, cols]


def split(value):
    high = value.astype(jnp.bfloat16)
    return high, (value - high.astype(jnp.float32)).astype(jnp.bfloat16)


def product(left, right):
    terms = ((0, 0), (0, 1), (1, 0))
    return sum(jnp.dot(left[i], right[j], preferred_element_type=jnp.float32) for i, j in terms)


def repeat_kernel(own, inverse, repeated):
    _, rows, span = repeated.shape
    cut = inverse.shape[0]
    repeated[0, :cut] = inverse[...]
    for block in range(rows - cut):
        value = own[block].astype(jnp.float32)
        repeated[0, cut + block : cut + block + 1] = jnp.full((1, span), value, jnp.float32)


def copy_kernel(inverse, repeated):
    repeated[0] = inverse[...]


def halve_kernel(value, high, low):
    high[...], low[...] = split(value[...])


def couple_kernel(slots, where, *rest):
    pieces, (high, low, placed) = rest[:9], rest[9:12]
    shares, (rows, total) = rest[12 : 12 + slots], rest[12 + slots :]
    step = pl.program_id(0)
    part = pieces[0].shape[2]
    tall = rows.shape[0] // (2 * part)
    level, core = where[2], where[3]
    way = 1 - 2 * core

    def put(piece, entry, distance, owner):
        at = lax.rem(level + distance + tall, tall)
        rows[pl.ds(pl.multiple_of((at * 2 + owner) * part, part), part)] = piece[entry, 0]

    own, near, far = pieces[0], pieces[1:4], pieces[4:7]
    put(own, 0, 0, core)
    put(own, 1, 0, 1 - core)
    for k in range(3):
        put(near[k], 0, -(k + 1) * way, core)
        put(near[k], 1, -(k + 1) * way, 1 - core)
        put(far[k], 0, (k + 1) * way, 1 - core)
        put(far[k], 1, (k + 1) * way, core)
    put(pieces[7], 0, tall // 2, core)
    put(pieces[8], 0, tall // 2, 1 - core)
    wide = placed.shape[2]
    total[...] = -product(split(rows[...]), (high[...], low[...]))
    window = pl.ds(pl.multiple_of(where[1] * BLK, BLK), wide)
    total[:, window] = total[:, window] + placed[0]
    half = total.shape[1] // 2
    across = slots // 2
    for slot in range(across):

        @pl.when(step == (slot + across - 1) % across)
        def _():
            shares[slot][...] = total[:, :half]
            shares[across + slot][...] = total[:, half:]


def join_kernel(pieces_a, pieces_b, copies):
    first, second = jnp.sum(pieces_a[...], axis=0), jnp.sum(pieces_b[...], axis=0)
    cut = first.shape[1]
    for level in range(copies.shape[0]):
        copies[level, :, :cut] = first
        copies[level, :, cut:] = second


def solve_kernel(core, reduced, inverse_lo, inverse_hi, kept, other, *parts):
    cut = inverse_lo.shape[1]

    @pl.when(pl.program_id(0) == 0)
    def _():
        for at, piece in enumerate((reduced[:, :cut], reduced[:, cut:])):
            parts[2 * at][...], parts[2 * at + 1][...] = split(piece)

    _, tall, part, span = kept.shape
    result = product((parts[0][...], parts[1][...]), split(inverse_lo[0]))
    result = result + product((parts[2][...], parts[3][...]), split(inverse_hi[0]))
    result = result.reshape(tall, 2, part, span)
    first, second = result[:, 0], result[:, 1]
    mine = core[0] == 0
    kept[0] = jnp.where(mine, first, second)
    other[0] = jnp.where(mine, second, first)


def child_kernel(first, length, pieces, children, summed):
    quarters, _, rows, span = pieces.shape
    padded = summed.shape[1]
    for quarter in range(quarters):
        own = slice(quarter * rows, (quarter + 1) * rows)
        summed[own, :span] = jnp.sum(pieces[quarter], axis=0)
    summed[:, span:] = jnp.zeros((quarters * rows, padded - span), jnp.float32)
    lane = lax.broadcasted_iota(jnp.int32, (quarters * rows, BLK), 1)
    for child in range(first.shape[0]):
        offset = jnp.clip(first[child], 0, span - 1)
        tile = lax.div(offset, BLK)
        window = summed[:, pl.ds(pl.multiple_of(tile * BLK, BLK), 2 * BLK)]
        shift = lax.rem(2 * BLK - (offset - tile * BLK), 2 * BLK)
        moved = pltpu.roll(window, shift, 1)[:, :BLK]
        children[:, child * BLK : (child + 1) * BLK] = jnp.where(
            lane < length[child], moved, jnp.zeros_like(moved)
        )


def body(ancestor_sol, front_map, lower_panel, inverse_factor, right_side, child_start, child_len):
    deep, across, tall, cores = (lax.axis_size(a) for a in ("z", "x", "y", "c"))
    srcs, width = ancestor_sol.shape
    count = front_map.shape[0]
    pivots, span = inverse_factor.shape
    total = right_side.shape[0]
    piv_devs = tall * cores
    part = srcs // across
    quarter = total // across
    me = lax.axis_index(ROWS)

    half = pivots // 2
    cut = pivots // 4
    core = lax.axis_index("c")
    first = child_start - me * span

    def ring(value, axis, hops):
        length = lax.axis_size(axis)
        return lax.ppermute(value, axis, [(i, (i + hops) % length) for i in range(length)])

    down_2, up_2 = ring(ancestor_sol, "z", 2), ring(ancestor_sol, "z", -2)
    down_1, up_1 = ring(ancestor_sol, "z", 1), ring(ancestor_sol, "z", -1)
    inverse_lo = pl.pallas_call(
        repeat_kernel,
        grid=(across,),
        out_shape=jax.ShapeDtypeStruct((across, cut + count, span), jnp.float32),
        in_specs=[SMEM, pl.BlockSpec((cut, span), lambda i: (0, 0))],
        out_specs=pl.BlockSpec((1, cut + count, span), lambda i: (i, 0, 0)),
        compiler_params=grant(60),
        name="repeat",
    )(front_map, inverse_factor)
    inverse_lo = exchange(inverse_lo, "x")
    maps = inverse_lo[:, cut:, 0].astype(jnp.int32)
    mid = srcs // 2
    upper, lower = ring(down_2[:mid], "z", 2), ring(up_2[mid:], "z", -2)
    down_3, up_3 = ring(down_2, "z", 1), ring(up_2, "z", -1)
    column = (ancestor_sol, up_1, up_2, up_3, down_3, down_2, down_1, upper, lower)
    column, maps, first = lax.optimization_barrier((column, maps, first))
    sends = pl.pallas_call(
        lambda *refs: pack_kernel(count, *refs),
        out_shape=jax.ShapeDtypeStruct((across, srcs, width), jnp.float32),
        in_specs=[SMEM, SMEM] + [VMEM] * len(column),
        out_specs=VMEM,
        scratch_shapes=[pltpu.VMEM((deep, srcs, width), jnp.float32)],
        compiler_params=grant(12),
        name="pack",
    )(maps, lax.axis_index("z").reshape(1), *column)
    sends, inverse_lo, inverse_factor, right_side, lower_panel = lax.optimization_barrier(
        (sends, inverse_lo, inverse_factor, right_side, lower_panel)
    )
    arrived = exchange(sends, "x")
    rest = pl.pallas_call(
        copy_kernel,
        grid=(pivots // cut - 1, across),
        out_shape=jax.ShapeDtypeStruct((across, pivots - cut, span), jnp.float32),
        in_specs=[pl.BlockSpec((cut, span), lambda j, i: (j + 1, 0))],
        out_specs=pl.BlockSpec((1, cut, span), lambda j, i: (i, j, 0)),
        compiler_params=grant(60),
        cost_estimate=pl.CostEstimate(
            flops=pivots * span, bytes_accessed=5 * 4 * pivots * span, transcendentals=0
        ),
        name="copies",
    )(inverse_factor)
    panel_high, panel_low = pl.pallas_call(
        halve_kernel,
        grid=(4,),
        out_shape=(jax.ShapeDtypeStruct((width, pivots), jnp.bfloat16),) * 2,
        in_specs=[pl.BlockSpec((width // 4, pivots), lambda i: (i, 0))],
        out_specs=(pl.BlockSpec((width // 4, pivots), lambda i: (i, 0)),) * 2,
        compiler_params=grant(60),
        cost_estimate=pl.CostEstimate(
            flops=4 * width * pivots, bytes_accessed=8 * width * pivots, transcendentals=0
        ),
        name="halve",
    )(lower_panel)
    own_share = right_side.shape[1]
    tile = jnp.minimum(lax.div(me * own_share, BLK), pivots // BLK - 2)
    place = (
        jnp.arange(2 * BLK, dtype=jnp.int32)[None, :]
        == me * own_share - tile * BLK + jnp.arange(own_share, dtype=jnp.int32)[:, None]
    ).astype(jnp.float32)
    ordered = right_side.reshape(piv_devs, across, part, own_share).swapaxes(0, 1)
    placed = jnp.dot(
        ordered.reshape(total, own_share),
        place,
        precision=lax.Precision.HIGHEST,
        preferred_element_type=jnp.float32,
    ).reshape(across, quarter, 2 * BLK)
    boundary = pl.pallas_call(
        lambda *refs: pick_kernel(count, *refs),
        out_shape=jax.ShapeDtypeStruct((srcs, width), jnp.float32),
        in_specs=[SMEM, VMEM],
        out_specs=VMEM,
        compiler_params=grant(8),
        name="pick",
    )(front_map, arrived)
    boundary, rest, placed, panel_high, panel_low = lax.optimization_barrier(
        (boundary, rest, placed, panel_high, panel_low)
    )

    def swap(value):
        return lax.ppermute(value, "c", [(0, 1), (1, 0)])

    def apart(value, hops):
        pairs = [
            (2 * y + c, 2 * ((y + (hops, -hops)[c]) % tall) + c)
            for y in range(tall)
            for c in range(cores)
        ]
        return lax.ppermute(value, PIV, pairs)

    chip = jnp.stack([boundary, swap(boundary)])
    near_2, near_1 = apart(chip, 2), apart(chip, 1)
    inverse_hi = exchange(rest, "x")
    near_4, near_3 = apart(near_2[0], 2), apart(near_2, 1)
    far_2, far_1, far_4, far_3 = swap(near_2), swap(near_1), swap(near_4), swap(near_3)
    pieces = (chip, near_1, near_2, near_3, far_1, far_2, far_3, near_4, far_4)
    pieces = [piece.reshape(-1, across, part, width) for piece in pieces]
    few = quarter // deep
    where = jnp.stack([lax.axis_index("x"), tile, lax.axis_index("y"), core])

    def turn(i, at):
        return (lax.rem(at[0] + 1 + i, across), 0, 0)

    shares = pl.pallas_call(
        lambda *refs: couple_kernel(2 * across, *refs),
        grid_spec=pltpu.PrefetchScalarGridSpec(
            num_scalar_prefetch=1,
            grid=(across,),
            in_specs=[
                pl.BlockSpec(
                    (piece.shape[0], 1, part, width), lambda i, at: (0, turn(i, at)[0], 0, 0)
                )
                for piece in pieces
            ]
            + [
                pl.BlockSpec((width, pivots), lambda i, at: (0, 0)),
                pl.BlockSpec((width, pivots), lambda i, at: (0, 0)),
                pl.BlockSpec((1, quarter, 2 * BLK), turn),
            ],
            out_specs=(pl.BlockSpec((quarter, half), lambda i, at: (0, 0)),) * (2 * across),
            scratch_shapes=[
                pltpu.VMEM((quarter, width), jnp.float32),
                pltpu.VMEM((quarter, pivots), jnp.float32),
            ],
        ),
        out_shape=(jax.ShapeDtypeStruct((quarter, half), jnp.float32),) * (2 * across),
        compiler_params=grant(52),
        cost_estimate=pl.CostEstimate(
            flops=6 * total * width * pivots,
            bytes_accessed=4 * (total * width + width * pivots + total * pivots),
            transcendentals=0,
        ),
        name="couple",
    )(where, *pieces, panel_high, panel_low, placed)
    shares_a, shares_b = shares[:across], shares[across:]

    def across_sent(shares):
        return [
            lax.ppermute(shares[k], "x", [(i, (i + k) % across) for i in range(across)])
            for k in range(1, across)
        ]

    def nearer(shares, arrived):
        summed = shares[0] + sum(arrived[1:], arrived[0])
        return exchange(summed.reshape(deep, few, half), "z")

    arrived_a = across_sent(shares_a)
    arrived_b = across_sent(shares_b)
    own_a, inverse_hi = lax.optimization_barrier((shares_a[0], inverse_hi))
    shares_a = (own_a, *shares_a[1:])
    nearer_a = nearer(shares_a, arrived_a)
    own_b, nearer_a = lax.optimization_barrier((shares_b[0], nearer_a))
    shares_b = (own_b, *shares_b[1:])
    nearer_b = nearer(shares_b, arrived_b)
    copies = pl.pallas_call(
        join_kernel,
        out_shape=jax.ShapeDtypeStruct((deep, few, pivots), jnp.float32),
        in_specs=[VMEM, VMEM],
        out_specs=VMEM,
        compiler_params=grant(8),
        name="join",
    )(nearer_a, nearer_b)
    reduced = exchange(copies, "z").reshape(quarter, pivots)
    kept, other = pl.pallas_call(
        solve_kernel,
        grid=(across,),
        out_shape=(jax.ShapeDtypeStruct((across, tall, part, span), jnp.float32),) * 2,
        in_specs=[
            SMEM,
            pl.BlockSpec((quarter, pivots), lambda i: (0, 0)),
            pl.BlockSpec((1, cut, span), lambda i: (i, 0, 0)),
            pl.BlockSpec((1, pivots - cut, span), lambda i: (i, 0, 0)),
        ],
        out_specs=(pl.BlockSpec((1, tall, part, span), lambda i: (i, 0, 0, 0)),) * 2,
        scratch_shapes=[
            pltpu.VMEM((quarter, size), jnp.bfloat16)
            for size in (cut, cut, pivots - cut, pivots - cut)
        ],
        compiler_params=grant(60),
        name="solve",
    )(
        core.reshape(1),
        reduced,
        inverse_lo,
        inverse_hi,
    )
    kept = kept + swap(other)
    arrived = exchange(kept.reshape(across * tall, part, span), ("x", "y"))
    return pl.pallas_call(
        child_kernel,
        out_shape=jax.ShapeDtypeStruct((srcs, child_len.shape[0] * BLK), jnp.float32),
        in_specs=[SMEM, SMEM, VMEM],
        out_specs=VMEM,
        scratch_shapes=[pltpu.VMEM((srcs, span + BLK), jnp.float32)],
        compiler_params=grant(8),
        name="children",
    )(first, child_len, arrived.reshape(across, tall, part, span))


def solution(mesh):
    piv = mesh.shape["piv"]
    torus = Mesh(mesh.devices.reshape(8, 4, piv // 2, 2), ("z", "x", "y", "c"))
    return jax.shard_map(
        body,
        mesh=torus,
        in_specs=(
            P(PIV, ROWS),
            P(ROWS),
            P(ROWS, PIV),
            P(PIV, ROWS),
            P(None, PIV + ROWS),
            P(ROWS),
            P(ROWS),
        ),
        out_specs=P(PIV, ROWS),
        check_vma=False,
    )
```

```python
import jax
import jax.numpy as jnp
from jax import lax
from jax.experimental import pallas as pl
from jax.experimental.pallas import tpu as pltpu
from jax.sharding import Mesh
from jax.sharding import PartitionSpec as P

BLK = 128
ROWS = ("z", "x")
PIV = ("y", "c")
VMEM = pl.BlockSpec(memory_space=pltpu.VMEM)
SMEM = pl.BlockSpec(memory_space=pltpu.SMEM)


def grant(size):
    return pltpu.CompilerParams(vmem_limit_bytes=size << 20)


def exchange(value, axes):
    return lax.all_to_all(value, axes, split_axis=0, concat_axis=0, tiled=True)


def pack_kernel(count, maps, where, *rest):
    pieces, sends, column = rest[:-2], rest[-2], rest[-1]
    across, deep = maps.shape[0], column.shape[0]
    for level, piece in enumerate(pieces[:-2]):
        column[level if level < deep // 2 else level + 1] = piece[...]
    upper, lower = pieces[-2:]
    column[deep // 2, : upper.shape[0]] = upper[...]
    column[deep // 2, upper.shape[0] :] = lower[...]
    for dest in range(across):
        for slot in range(count):
            block = maps[dest, slot]
            level = lax.rem(lax.div(block, count * across) - where[0] + deep, deep)
            offset = pl.multiple_of(lax.rem(block, count) * BLK, BLK)
            sends[dest, :, slot * BLK : (slot + 1) * BLK] = column[level, :, pl.ds(offset, BLK)]


def pick_kernel(count, own, arrived, boundary):
    across = arrived.shape[0]
    for slot in range(count):
        origin = lax.rem(lax.div(own[slot], count), across)
        cols = slice(slot * BLK, (slot + 1) * BLK)
        boundary[:, cols] = arrived[origin, :, cols]


def split(value):
    high = value.astype(jnp.bfloat16)
    return high, (value - high.astype(jnp.float32)).astype(jnp.bfloat16)


def product(left, right):
    terms = ((0, 0), (0, 1), (1, 0))
    return sum(jnp.dot(left[i], right[j], preferred_element_type=jnp.float32) for i, j in terms)


def repeat_kernel(own, inverse, repeated):
    _, rows, span = repeated.shape
    cut = inverse.shape[0]
    repeated[0, :cut] = inverse[...]
    for block in range(rows - cut):
        value = own[block].astype(jnp.float32)
        repeated[0, cut + block : cut + block + 1] = jnp.full((1, span), value, jnp.float32)


def copy_kernel(inverse, repeated):
    repeated[0] = inverse[...]


def couple_kernel(slots, where, *rest):
    pieces, (panel, placed) = rest[:10], rest[10:12]
    shares, (rows, high, low, total) = rest[12 : 12 + slots], rest[12 + slots :]
    step = pl.program_id(0)

    @pl.when(step == 0)
    def _():
        high[...], low[...] = split(panel[...])

    part = pieces[0].shape[2]
    tall = rows.shape[0] // (2 * part)
    level, core = where[2], where[3]
    way = 1 - 2 * core

    def put(piece, entry, distance, owner):
        at = lax.rem(level + distance + tall, tall)
        rows[pl.ds(pl.multiple_of((at * 2 + owner) * part, part), part)] = piece[entry, 0]

    near, far = pieces[2:5], pieces[5:8]
    put(pieces[0], 0, 0, core)
    put(pieces[1], 0, 0, 1 - core)
    for k in range(3):
        put(near[k], 0, -(k + 1) * way, core)
        put(near[k], 1, -(k + 1) * way, 1 - core)
        put(far[k], 0, (k + 1) * way, 1 - core)
        put(far[k], 1, (k + 1) * way, core)
    put(pieces[8], 0, tall // 2, core)
    put(pieces[9], 0, tall // 2, 1 - core)
    wide = placed.shape[2]
    total[...] = -product(split(rows[...]), (high[...], low[...]))
    window = pl.ds(pl.multiple_of(where[1] * BLK, BLK), wide)
    total[:, window] = total[:, window] + placed[0]
    half = total.shape[1] // 2
    across = slots // 2
    for slot in range(across):

        @pl.when(step == (slot + across - 1) % across)
        def _():
            shares[slot][...] = total[:, :half]
            shares[across + slot][...] = total[:, half:]


def join_kernel(pieces_a, pieces_b, copies):
    first, second = jnp.sum(pieces_a[...], axis=0), jnp.sum(pieces_b[...], axis=0)
    cut = first.shape[1]
    for level in range(copies.shape[0]):
        copies[level, :, :cut] = first
        copies[level, :, cut:] = second


def solve_kernel(core, reduced, inverse_lo, inverse_hi, kept, other, *parts):
    cut = inverse_lo.shape[1]

    @pl.when(pl.program_id(0) == 0)
    def _():
        for at, piece in enumerate((reduced[:, :cut], reduced[:, cut:])):
            parts[2 * at][...], parts[2 * at + 1][...] = split(piece)

    _, tall, part, span = kept.shape
    result = product((parts[0][...], parts[1][...]), split(inverse_lo[0]))
    result = result + product((parts[2][...], parts[3][...]), split(inverse_hi[0]))
    result = result.reshape(tall, 2, part, span)
    first, second = result[:, 0], result[:, 1]
    mine = core[0] == 0
    kept[0] = jnp.where(mine, first, second)
    other[0] = jnp.where(mine, second, first)


def child_kernel(first, length, pieces, children, summed):
    quarters, _, rows, span = pieces.shape
    padded = summed.shape[1]
    for quarter in range(quarters):
        own = slice(quarter * rows, (quarter + 1) * rows)
        summed[own, :span] = jnp.sum(pieces[quarter], axis=0)
    summed[:, span:] = jnp.zeros((quarters * rows, padded - span), jnp.float32)
    lane = lax.broadcasted_iota(jnp.int32, (quarters * rows, BLK), 1)
    for child in range(first.shape[0]):
        offset = jnp.clip(first[child], 0, span - 1)
        tile = lax.div(offset, BLK)
        window = summed[:, pl.ds(pl.multiple_of(tile * BLK, BLK), 2 * BLK)]
        shift = lax.rem(2 * BLK - (offset - tile * BLK), 2 * BLK)
        moved = pltpu.roll(window, shift, 1)[:, :BLK]
        children[:, child * BLK : (child + 1) * BLK] = jnp.where(
            lane < length[child], moved, jnp.zeros_like(moved)
        )


def body(ancestor_sol, front_map, lower_panel, inverse_factor, right_side, child_start, child_len):
    deep, across, tall, cores = (lax.axis_size(a) for a in ("z", "x", "y", "c"))
    srcs, width = ancestor_sol.shape
    count = front_map.shape[0]
    pivots, span = inverse_factor.shape
    total = right_side.shape[0]
    piv_devs = tall * cores
    part = srcs // across
    quarter = total // across
    me = lax.axis_index(ROWS)

    half = pivots // 2
    cut = pivots // 4
    core = lax.axis_index("c")
    first = child_start - me * span

    def ring(value, axis, hops):
        length = lax.axis_size(axis)
        return lax.ppermute(value, axis, [(i, (i + hops) % length) for i in range(length)])

    down_2, up_2 = ring(ancestor_sol, "z", 2), ring(ancestor_sol, "z", -2)
    down_1, up_1 = ring(ancestor_sol, "z", 1), ring(ancestor_sol, "z", -1)
    inverse_lo = pl.pallas_call(
        repeat_kernel,
        grid=(across,),
        out_shape=jax.ShapeDtypeStruct((across, cut + count, span), jnp.float32),
        in_specs=[SMEM, pl.BlockSpec((cut, span), lambda i: (0, 0))],
        out_specs=pl.BlockSpec((1, cut + count, span), lambda i: (i, 0, 0)),
        compiler_params=grant(60),
        name="repeat",
    )(front_map, inverse_factor)
    inverse_lo = exchange(inverse_lo, "x")
    maps = inverse_lo[:, cut:, 0].astype(jnp.int32)
    mid = srcs // 2
    upper, lower = ring(down_2[:mid], "z", 2), ring(up_2[mid:], "z", -2)
    down_3, up_3 = ring(down_2, "z", 1), ring(up_2, "z", -1)
    column = (ancestor_sol, up_1, up_2, up_3, down_3, down_2, down_1, upper, lower)
    column, maps, first = lax.optimization_barrier((column, maps, first))
    sends = pl.pallas_call(
        lambda *refs: pack_kernel(count, *refs),
        out_shape=jax.ShapeDtypeStruct((across, srcs, width), jnp.float32),
        in_specs=[SMEM, SMEM] + [VMEM] * len(column),
        out_specs=VMEM,
        scratch_shapes=[pltpu.VMEM((deep, srcs, width), jnp.float32)],
        compiler_params=grant(12),
        name="pack",
    )(maps, lax.axis_index("z").reshape(1), *column)
    sends, inverse_lo, inverse_factor, right_side = lax.optimization_barrier(
        (sends, inverse_lo, inverse_factor, right_side)
    )
    arrived = exchange(sends, "x")
    rest = pl.pallas_call(
        copy_kernel,
        grid=(pivots // cut - 1, across),
        out_shape=jax.ShapeDtypeStruct((across, pivots - cut, span), jnp.float32),
        in_specs=[pl.BlockSpec((cut, span), lambda j, i: (j + 1, 0))],
        out_specs=pl.BlockSpec((1, cut, span), lambda j, i: (i, j, 0)),
        compiler_params=grant(60),
        cost_estimate=pl.CostEstimate(
            flops=pivots * span, bytes_accessed=5 * 4 * pivots * span, transcendentals=0
        ),
        name="copies",
    )(inverse_factor)
    own_share = right_side.shape[1]
    tile = jnp.minimum(lax.div(me * own_share, BLK), pivots // BLK - 2)
    place = (
        jnp.arange(2 * BLK, dtype=jnp.int32)[None, :]
        == me * own_share - tile * BLK + jnp.arange(own_share, dtype=jnp.int32)[:, None]
    ).astype(jnp.float32)
    ordered = right_side.reshape(piv_devs, across, part, own_share).swapaxes(0, 1)
    placed = jnp.dot(
        ordered.reshape(total, own_share),
        place,
        precision=lax.Precision.HIGHEST,
        preferred_element_type=jnp.float32,
    ).reshape(across, quarter, 2 * BLK)
    boundary = pl.pallas_call(
        lambda *refs: pick_kernel(count, *refs),
        out_shape=jax.ShapeDtypeStruct((srcs, width), jnp.float32),
        in_specs=[SMEM, VMEM],
        out_specs=VMEM,
        compiler_params=grant(8),
        name="pick",
    )(front_map, arrived)
    boundary, rest, placed = lax.optimization_barrier((boundary, rest, placed))

    def swap(value):
        return lax.ppermute(value, "c", [(0, 1), (1, 0)])

    def apart(value, hops):
        pairs = [
            (2 * y + c, 2 * ((y + (hops, -hops)[c]) % tall) + c)
            for y in range(tall)
            for c in range(cores)
        ]
        return lax.ppermute(value, PIV, pairs)

    partner = swap(boundary)
    chip = jnp.stack([boundary, partner])
    near_2, near_1 = apart(chip, 2), apart(chip, 1)
    inverse_hi = exchange(rest, "x")
    near_4, near_3 = apart(near_2[0], 2), apart(near_2, 1)
    far_2, far_1, far_4, far_3 = swap(near_2), swap(near_1), swap(near_4), swap(near_3)
    pieces = (boundary, partner, near_1, near_2, near_3, far_1, far_2, far_3, near_4, far_4)
    pieces = [piece.reshape(-1, across, part, width) for piece in pieces]
    few = quarter // deep
    where = jnp.stack([lax.axis_index("x"), tile, lax.axis_index("y"), core])

    def turn(i, at):
        return (lax.rem(at[0] + 1 + i, across), 0, 0)

    shares = pl.pallas_call(
        lambda *refs: couple_kernel(2 * across, *refs),
        grid_spec=pltpu.PrefetchScalarGridSpec(
            num_scalar_prefetch=1,
            grid=(across,),
            in_specs=[
                pl.BlockSpec(
                    (piece.shape[0], 1, part, width), lambda i, at: (0, turn(i, at)[0], 0, 0)
                )
                for piece in pieces
            ]
            + [
                pl.BlockSpec((width, pivots), lambda i, at: (0, 0)),
                pl.BlockSpec((1, quarter, 2 * BLK), turn),
            ],
            out_specs=(pl.BlockSpec((quarter, half), lambda i, at: (0, 0)),) * (2 * across),
            scratch_shapes=[
                pltpu.VMEM((quarter, width), jnp.float32),
                pltpu.VMEM((width, pivots), jnp.bfloat16),
                pltpu.VMEM((width, pivots), jnp.bfloat16),
                pltpu.VMEM((quarter, pivots), jnp.float32),
            ],
        ),
        out_shape=(jax.ShapeDtypeStruct((quarter, half), jnp.float32),) * (2 * across),
        compiler_params=grant(52),
        cost_estimate=pl.CostEstimate(
            flops=6 * total * width * pivots,
            bytes_accessed=4 * (total * width + width * pivots + total * pivots),
            transcendentals=0,
        ),
        name="couple",
    )(where, *pieces, lower_panel, placed)
    shares_a, shares_b = shares[:across], shares[across:]

    def across_sent(shares):
        return [
            lax.ppermute(shares[k], "x", [(i, (i + k) % across) for i in range(across)])
            for k in range(1, across)
        ]

    def nearer(shares, arrived):
        summed = shares[0] + sum(arrived[1:], arrived[0])
        return exchange(summed.reshape(deep, few, half), "z")

    arrived_a = across_sent(shares_a)
    arrived_b = across_sent(shares_b)
    own_a, inverse_hi = lax.optimization_barrier((shares_a[0], inverse_hi))
    shares_a = (own_a, *shares_a[1:])
    nearer_a = nearer(shares_a, arrived_a)
    own_b, nearer_a = lax.optimization_barrier((shares_b[0], nearer_a))
    shares_b = (own_b, *shares_b[1:])
    nearer_b = nearer(shares_b, arrived_b)
    copies = pl.pallas_call(
        join_kernel,
        out_shape=jax.ShapeDtypeStruct((deep, few, pivots), jnp.float32),
        in_specs=[VMEM, VMEM],
        out_specs=VMEM,
        compiler_params=grant(8),
        name="join",
    )(nearer_a, nearer_b)
    reduced = exchange(copies, "z").reshape(quarter, pivots)
    kept, other = pl.pallas_call(
        solve_kernel,
        grid=(across,),
        out_shape=(jax.ShapeDtypeStruct((across, tall, part, span), jnp.float32),) * 2,
        in_specs=[
            SMEM,
            pl.BlockSpec((quarter, pivots), lambda i: (0, 0)),
            pl.BlockSpec((1, cut, span), lambda i: (i, 0, 0)),
            pl.BlockSpec((1, pivots - cut, span), lambda i: (i, 0, 0)),
        ],
        out_specs=(pl.BlockSpec((1, tall, part, span), lambda i: (i, 0, 0, 0)),) * 2,
        scratch_shapes=[
            pltpu.VMEM((quarter, size), jnp.bfloat16)
            for size in (cut, cut, pivots - cut, pivots - cut)
        ],
        compiler_params=grant(60),
        name="solve",
    )(
        core.reshape(1),
        reduced,
        inverse_lo,
        inverse_hi,
    )
    kept = kept + swap(other)
    arrived = exchange(kept.reshape(across * tall, part, span), ("x", "y"))
    return pl.pallas_call(
        child_kernel,
        out_shape=jax.ShapeDtypeStruct((srcs, child_len.shape[0] * BLK), jnp.float32),
        in_specs=[SMEM, SMEM, VMEM],
        out_specs=VMEM,
        scratch_shapes=[pltpu.VMEM((srcs, span + BLK), jnp.float32)],
        compiler_params=grant(8),
        name="children",
    )(first, child_len, arrived.reshape(across, tall, part, span))


def solution(mesh):
    piv = mesh.shape["piv"]
    torus = Mesh(mesh.devices.reshape(8, 4, piv // 2, 2), ("z", "x", "y", "c"))
    return jax.shard_map(
        body,
        mesh=torus,
        in_specs=(
            P(PIV, ROWS),
            P(ROWS),
            P(ROWS, PIV),
            P(PIV, ROWS),
            P(None, PIV + ROWS),
            P(ROWS),
            P(ROWS),
        ),
        out_specs=P(PIV, ROWS),
        check_vma=False,
    )
```

```python
import jax
import jax.numpy as jnp
from jax import lax
from jax.experimental import pallas as pl
from jax.experimental.pallas import tpu as pltpu
from jax.sharding import Mesh
from jax.sharding import PartitionSpec as P

BLK = 128
ROWS = ("z", "x")
PIV = ("y", "c")
VMEM = pl.BlockSpec(memory_space=pltpu.VMEM)
SMEM = pl.BlockSpec(memory_space=pltpu.SMEM)


def grant(size):
    return pltpu.CompilerParams(vmem_limit_bytes=size << 20)


def exchange(value, axes):
    return lax.all_to_all(value, axes, split_axis=0, concat_axis=0, tiled=True)


def pack_kernel(count, maps, where, *rest):
    pieces, sends, column = rest[:-2], rest[-2], rest[-1]
    across, deep = maps.shape[0], column.shape[0]
    for level, piece in enumerate(pieces[:-2]):
        column[level if level < deep // 2 else level + 1] = piece[...]
    upper, lower = pieces[-2:]
    column[deep // 2, : upper.shape[0]] = upper[...]
    column[deep // 2, upper.shape[0] :] = lower[...]
    for dest in range(across):
        for slot in range(count):
            block = maps[dest, slot]
            level = lax.rem(lax.div(block, count * across) - where[0] + deep, deep)
            offset = pl.multiple_of(lax.rem(block, count) * BLK, BLK)
            sends[dest, :, slot * BLK : (slot + 1) * BLK] = column[level, :, pl.ds(offset, BLK)]


def pick_kernel(count, own, arrived, boundary):
    across = arrived.shape[0]
    for slot in range(count):
        origin = lax.rem(lax.div(own[slot], count), across)
        cols = slice(slot * BLK, (slot + 1) * BLK)
        boundary[:, cols] = arrived[origin, :, cols]


def split(value):
    high = value.astype(jnp.bfloat16)
    return high, (value - high.astype(jnp.float32)).astype(jnp.bfloat16)


def product(left, right):
    terms = ((0, 0), (0, 1), (1, 0))
    return sum(jnp.dot(left[i], right[j], preferred_element_type=jnp.float32) for i, j in terms)


def repeat_kernel(own, inverse, repeated):
    _, rows, span = repeated.shape
    cut = inverse.shape[0]
    repeated[0, :cut] = inverse[...]
    for block in range(rows - cut):
        value = own[block].astype(jnp.float32)
        repeated[0, cut + block : cut + block + 1] = jnp.full((1, span), value, jnp.float32)


def copy_kernel(inverse, repeated):
    repeated[0] = inverse[...]


def couple_kernel(slots, where, *rest):
    pieces, (panel, placed) = rest[:10], rest[10:12]
    shares, (rows, high, low, total) = rest[12 : 12 + slots], rest[12 + slots :]
    step = pl.program_id(0)

    @pl.when(step == 0)
    def _():
        high[...], low[...] = split(panel[...])

    part = pieces[0].shape[2]
    tall = rows.shape[0] // (2 * part)
    level, core = where[2], where[3]
    way = 1 - 2 * core

    def put(piece, entry, distance, owner):
        at = lax.rem(level + distance + tall, tall)
        rows[pl.ds(pl.multiple_of((at * 2 + owner) * part, part), part)] = piece[entry, 0]

    near, far = pieces[2:5], pieces[5:8]
    put(pieces[0], 0, 0, core)
    put(pieces[1], 0, 0, 1 - core)
    for k in range(3):
        put(near[k], 0, -(k + 1) * way, core)
        put(near[k], 1, -(k + 1) * way, 1 - core)
        put(far[k], 0, (k + 1) * way, 1 - core)
        put(far[k], 1, (k + 1) * way, core)
    put(pieces[8], 0, tall // 2, core)
    put(pieces[9], 0, tall // 2, 1 - core)
    wide = placed.shape[2]
    total[...] = -product(split(rows[...]), (high[...], low[...]))
    window = pl.ds(pl.multiple_of(where[1] * BLK, BLK), wide)
    total[:, window] = total[:, window] + placed[0]
    half = shares[0].shape[1]
    across = slots // 2
    for slot in range(across):

        @pl.when(step == (slot + across - 1) % across)
        def _():
            shares[slot][...] = total[:, :half]
            shares[across + slot][...] = total[:, half:]


def join_kernel(pieces_a, pieces_b, copies):
    first, second = jnp.sum(pieces_a[...], axis=0), jnp.sum(pieces_b[...], axis=0)
    cut = first.shape[1]
    for level in range(copies.shape[0]):
        copies[level, :, :cut] = first
        copies[level, :, cut:] = second


def solve_kernel(core, reduced, inverse_lo, inverse_hi, kept, other, *parts):
    cut = inverse_lo.shape[1]

    @pl.when(pl.program_id(0) == 0)
    def _():
        for at, piece in enumerate((reduced[:, :cut], reduced[:, cut:])):
            parts[2 * at][...], parts[2 * at + 1][...] = split(piece)

    _, tall, part, span = kept.shape
    result = product((parts[0][...], parts[1][...]), split(inverse_lo[0]))
    result = result + product((parts[2][...], parts[3][...]), split(inverse_hi[0]))
    result = result.reshape(tall, 2, part, span)
    first, second = result[:, 0], result[:, 1]
    mine = core[0] == 0
    kept[0] = jnp.where(mine, first, second)
    other[0] = jnp.where(mine, second, first)


def child_kernel(first, length, pieces, children, summed):
    quarters, _, rows, span = pieces.shape
    padded = summed.shape[1]
    for quarter in range(quarters):
        own = slice(quarter * rows, (quarter + 1) * rows)
        summed[own, :span] = jnp.sum(pieces[quarter], axis=0)
    summed[:, span:] = jnp.zeros((quarters * rows, padded - span), jnp.float32)
    lane = lax.broadcasted_iota(jnp.int32, (quarters * rows, BLK), 1)
    for child in range(first.shape[0]):
        offset = jnp.clip(first[child], 0, span - 1)
        tile = lax.div(offset, BLK)
        window = summed[:, pl.ds(pl.multiple_of(tile * BLK, BLK), 2 * BLK)]
        shift = lax.rem(2 * BLK - (offset - tile * BLK), 2 * BLK)
        moved = pltpu.roll(window, shift, 1)[:, :BLK]
        children[:, child * BLK : (child + 1) * BLK] = jnp.where(
            lane < length[child], moved, jnp.zeros_like(moved)
        )


def body(ancestor_sol, front_map, lower_panel, inverse_factor, right_side, child_start, child_len):
    deep, across, tall, cores = (lax.axis_size(a) for a in ("z", "x", "y", "c"))
    srcs, width = ancestor_sol.shape
    count = front_map.shape[0]
    pivots, span = inverse_factor.shape
    total = right_side.shape[0]
    piv_devs = tall * cores
    part = srcs // across
    quarter = total // across
    me = lax.axis_index(ROWS)

    cut = pivots // 4
    core = lax.axis_index("c")
    first = child_start - me * span

    def ring(value, axis, hops):
        length = lax.axis_size(axis)
        return lax.ppermute(value, axis, [(i, (i + hops) % length) for i in range(length)])

    down_2, up_2 = ring(ancestor_sol, "z", 2), ring(ancestor_sol, "z", -2)
    down_1, up_1 = ring(ancestor_sol, "z", 1), ring(ancestor_sol, "z", -1)
    inverse_lo = pl.pallas_call(
        repeat_kernel,
        grid=(across,),
        out_shape=jax.ShapeDtypeStruct((across, cut + count, span), jnp.float32),
        in_specs=[SMEM, pl.BlockSpec((cut, span), lambda i: (0, 0))],
        out_specs=pl.BlockSpec((1, cut + count, span), lambda i: (i, 0, 0)),
        compiler_params=grant(60),
        name="repeat",
    )(front_map, inverse_factor)
    inverse_lo = exchange(inverse_lo, "x")
    maps = inverse_lo[:, cut:, 0].astype(jnp.int32)
    mid = srcs // 2
    upper, lower = ring(down_2[:mid], "z", 2), ring(up_2[mid:], "z", -2)
    down_3, up_3 = ring(down_2, "z", 1), ring(up_2, "z", -1)
    column = (ancestor_sol, up_1, up_2, up_3, down_3, down_2, down_1, upper, lower)
    column, maps, first = lax.optimization_barrier((column, maps, first))
    sends = pl.pallas_call(
        lambda *refs: pack_kernel(count, *refs),
        out_shape=jax.ShapeDtypeStruct((across, srcs, width), jnp.float32),
        in_specs=[SMEM, SMEM] + [VMEM] * len(column),
        out_specs=VMEM,
        scratch_shapes=[pltpu.VMEM((deep, srcs, width), jnp.float32)],
        compiler_params=grant(12),
        name="pack",
    )(maps, lax.axis_index("z").reshape(1), *column)
    sends, inverse_lo, inverse_factor, right_side = lax.optimization_barrier(
        (sends, inverse_lo, inverse_factor, right_side)
    )
    arrived = exchange(sends, "x")
    rest = pl.pallas_call(
        copy_kernel,
        grid=(pivots // cut - 1, across),
        out_shape=jax.ShapeDtypeStruct((across, pivots - cut, span), jnp.float32),
        in_specs=[pl.BlockSpec((cut, span), lambda j, i: (j + 1, 0))],
        out_specs=pl.BlockSpec((1, cut, span), lambda j, i: (i, j, 0)),
        compiler_params=grant(60),
        cost_estimate=pl.CostEstimate(
            flops=pivots * span, bytes_accessed=5 * 4 * pivots * span, transcendentals=0
        ),
        name="copies",
    )(inverse_factor)
    own_share = right_side.shape[1]
    tile = jnp.minimum(lax.div(me * own_share, BLK), pivots // BLK - 2)
    place = (
        jnp.arange(2 * BLK, dtype=jnp.int32)[None, :]
        == me * own_share - tile * BLK + jnp.arange(own_share, dtype=jnp.int32)[:, None]
    ).astype(jnp.float32)
    ordered = right_side.reshape(piv_devs, across, part, own_share).swapaxes(0, 1)
    placed = jnp.dot(
        ordered.reshape(total, own_share),
        place,
        precision=lax.Precision.HIGHEST,
        preferred_element_type=jnp.float32,
    ).reshape(across, quarter, 2 * BLK)
    boundary = pl.pallas_call(
        lambda *refs: pick_kernel(count, *refs),
        out_shape=jax.ShapeDtypeStruct((srcs, width), jnp.float32),
        in_specs=[SMEM, VMEM],
        out_specs=VMEM,
        compiler_params=grant(8),
        name="pick",
    )(front_map, arrived)
    boundary, rest, placed = lax.optimization_barrier((boundary, rest, placed))

    def swap(value):
        return lax.ppermute(value, "c", [(0, 1), (1, 0)])

    def apart(value, hops):
        pairs = [
            (2 * y + c, 2 * ((y + (hops, -hops)[c]) % tall) + c)
            for y in range(tall)
            for c in range(cores)
        ]
        return lax.ppermute(value, PIV, pairs)

    partner = swap(boundary)
    chip = jnp.stack([boundary, partner])
    near_2, near_1 = apart(chip, 2), apart(chip, 1)
    inverse_hi = exchange(rest, "x")
    near_4, near_3 = apart(near_2[0], 2), apart(near_2, 1)
    far_2, far_1, far_4, far_3 = swap(near_2), swap(near_1), swap(near_4), swap(near_3)
    pieces = (boundary, partner, near_1, near_2, near_3, far_1, far_2, far_3, near_4, far_4)
    pieces = [piece.reshape(-1, across, part, width) for piece in pieces]
    few = quarter // deep
    sizes = [pivots // 3] * across + [pivots - pivots // 3] * across
    where = jnp.stack([lax.axis_index("x"), tile, lax.axis_index("y"), core])

    def turn(i, at):
        return (lax.rem(at[0] + 1 + i, across), 0, 0)

    shares = pl.pallas_call(
        lambda *refs: couple_kernel(2 * across, *refs),
        grid_spec=pltpu.PrefetchScalarGridSpec(
            num_scalar_prefetch=1,
            grid=(across,),
            in_specs=[
                pl.BlockSpec(
                    (piece.shape[0], 1, part, width), lambda i, at: (0, turn(i, at)[0], 0, 0)
                )
                for piece in pieces
            ]
            + [
                pl.BlockSpec((width, pivots), lambda i, at: (0, 0)),
                pl.BlockSpec((1, quarter, 2 * BLK), turn),
            ],
            out_specs=[pl.BlockSpec((quarter, size), lambda i, at: (0, 0)) for size in sizes],
            scratch_shapes=[
                pltpu.VMEM((quarter, width), jnp.float32),
                pltpu.VMEM((width, pivots), jnp.bfloat16),
                pltpu.VMEM((width, pivots), jnp.bfloat16),
                pltpu.VMEM((quarter, pivots), jnp.float32),
            ],
        ),
        out_shape=[jax.ShapeDtypeStruct((quarter, size), jnp.float32) for size in sizes],
        compiler_params=grant(52),
        cost_estimate=pl.CostEstimate(
            flops=6 * total * width * pivots,
            bytes_accessed=4 * (total * width + width * pivots + total * pivots),
            transcendentals=0,
        ),
        name="couple",
    )(where, *pieces, lower_panel, placed)
    shares_a, shares_b = shares[:across], shares[across:]

    def across_sent(shares):
        return [
            lax.ppermute(shares[k], "x", [(i, (i + k) % across) for i in range(across)])
            for k in range(1, across)
        ]

    def nearer(shares, arrived):
        summed = shares[0] + sum(arrived[1:], arrived[0])
        return exchange(summed.reshape(deep, few, -1), "z")

    arrived_a = across_sent(shares_a)
    arrived_b = across_sent(shares_b)
    own_a, inverse_hi = lax.optimization_barrier((shares_a[0], inverse_hi))
    shares_a = (own_a, *shares_a[1:])
    nearer_a = nearer(shares_a, arrived_a)
    own_b, nearer_a = lax.optimization_barrier((shares_b[0], nearer_a))
    shares_b = (own_b, *shares_b[1:])
    nearer_b = nearer(shares_b, arrived_b)
    copies = pl.pallas_call(
        join_kernel,
        out_shape=jax.ShapeDtypeStruct((deep, few, pivots), jnp.float32),
        in_specs=[VMEM, VMEM],
        out_specs=VMEM,
        compiler_params=grant(8),
        name="join",
    )(nearer_a, nearer_b)
    reduced = exchange(copies, "z").reshape(quarter, pivots)
    kept, other = pl.pallas_call(
        solve_kernel,
        grid=(across,),
        out_shape=(jax.ShapeDtypeStruct((across, tall, part, span), jnp.float32),) * 2,
        in_specs=[
            SMEM,
            pl.BlockSpec((quarter, pivots), lambda i: (0, 0)),
            pl.BlockSpec((1, cut, span), lambda i: (i, 0, 0)),
            pl.BlockSpec((1, pivots - cut, span), lambda i: (i, 0, 0)),
        ],
        out_specs=(pl.BlockSpec((1, tall, part, span), lambda i: (i, 0, 0, 0)),) * 2,
        scratch_shapes=[
            pltpu.VMEM((quarter, size), jnp.bfloat16)
            for size in (cut, cut, pivots - cut, pivots - cut)
        ],
        compiler_params=grant(60),
        name="solve",
    )(
        core.reshape(1),
        reduced,
        inverse_lo,
        inverse_hi,
    )
    kept = kept + swap(other)
    arrived = exchange(kept.reshape(across * tall, part, span), ("x", "y"))
    return pl.pallas_call(
        child_kernel,
        out_shape=jax.ShapeDtypeStruct((srcs, child_len.shape[0] * BLK), jnp.float32),
        in_specs=[SMEM, SMEM, VMEM],
        out_specs=VMEM,
        scratch_shapes=[pltpu.VMEM((srcs, span + BLK), jnp.float32)],
        compiler_params=grant(8),
        name="children",
    )(first, child_len, arrived.reshape(across, tall, part, span))


def solution(mesh):
    piv = mesh.shape["piv"]
    torus = Mesh(mesh.devices.reshape(8, 4, piv // 2, 2), ("z", "x", "y", "c"))
    return jax.shard_map(
        body,
        mesh=torus,
        in_specs=(
            P(PIV, ROWS),
            P(ROWS),
            P(ROWS, PIV),
            P(PIV, ROWS),
            P(None, PIV + ROWS),
            P(ROWS),
            P(ROWS),
        ),
        out_specs=P(PIV, ROWS),
        check_vma=False,
    )
```
